256 devices in a mesh: section: 8 (over z), seq: 32 (over x, y, core).
Axes of the slice: x: 4, y: 4, z: 8, core: 2. Of those that a mesh axis runs over, the one named last changes fastest.
Arguments:
- section_input: bfloat16 [8, 8192, 1024], P('section', 'seq'), may hold values from -6 to 6
- stashed_input: bfloat16 [8, 8192, 1024], P('section', 'seq'), may hold values from -6 to 6
- output_grad: bfloat16 [8, 8192, 1024], P('section', 'seq'), may hold values from -6 to 6
- gain_mixer: float32 [8, 1024], P('section'), may hold values from 0.1 to 1.9
- gain_channel: float32 [8, 1024], P('section'), may hold values from 0.1 to 1.9
- factor_first: bfloat16 [8, 64, 128, 128], P('section', 'seq'), may hold values from -0.5 to 0.5
- factor_second: bfloat16 [8, 128, 64, 64], P('section', 'seq'), may hold values from -0.75 to 0.75
- spectrum: bfloat16 [8, 64, 128, 1024], P('section', None, 'seq'), may hold values from -6 to 6
- factor_third: bfloat16 [8, 128, 64, 64], P('section', 'seq'), may hold values from -0.75 to 0.75
- factor_fourth: bfloat16 [8, 64, 128, 128], P('section', 'seq'), may hold values from -0.5 to 0.5
- mixer_gate: bfloat16 [8, 1024, 256], P('section'), may hold values from -0.375 to 0.375
- channel_up: bfloat16 [8, 1024, 512], P('section'), may hold values from -0.375 to 0.375
- channel_gate: bfloat16 [8, 1024, 512], P('section'), may hold values from -0.375 to 0.375
- channel_down: bfloat16 [8, 2048, 256], P('section'), may hold values from -0.25 to 0.25
Outputs:
- next_input: bfloat16 [8, 8192, 1024], P('section', 'seq')
- upstream_grad: bfloat16 [8, 8192, 1024], P('section', 'seq')
- spectrum_grad: bfloat16 [8, 64, 128, 1024], P('section', None, 'seq')
- mixer_gate_grad: bfloat16 [8, 1024, 256], P('section', 'seq')
- channel_up_grad: bfloat16 [8, 1024, 512], P('section', 'seq')
- channel_gate_grad: bfloat16 [8, 1024, 512], P('section', 'seq')
- channel_down_grad: bfloat16 [8, 2048, 256], P('section', 'seq')
The draws below stay inside these ranges and needn't reach their ends.
All inputs are finite; a program needn't handle non-finite values.
Results may differ from the reference program's by a relative error of at most 0.017.
Values may be sent and summed in bfloat16 or wider, within the bound.
No kernel may reach another device: no remote copies, remote signals or barrier semaphores. Data moves between devices by JAX's collectives and lax.ppermute only.
A program may use at most 128 MiB of HBM per device.

```python
import math
import jax
import jax.numpy as jnp
from jax import lax

D = 1024
FF = 2048
NB = 4
NI = 64
NJ = 128
L = 8192
SECTIONS = 8
N_SECTION = 8


def strengthened(values, stream_key, source, target, blocks, factor):
    def block_of(axis_at):
        return (jnp.arange(values.shape[axis_at]) // (values.shape[axis_at] // blocks)).reshape((-1,) + (1,) * (values.ndim - 1 - axis_at))

    one_side = jax.random.permutation(stream_key, blocks)[block_of(target)]
    second = (block_of(target) + blocks // 2) % blocks
    return jnp.where((block_of(source) == one_side) | (block_of(source) == second), factor * values, values)


def level_of(key, shape, pieces, smallest, top_value):
    def one(dim, shards_of):
        heights = jax.random.uniform(jax.random.fold_in(jax.random.fold_in(key, 6), dim), (shards_of,), jnp.float32, smallest / len(pieces), top_value / len(pieces))
        return jnp.repeat(jnp.exp(heights), shape[dim] // shards_of).reshape((-1,) + (1,) * (len(shape) - dim - 1))

    loudness = one(*pieces[0])
    for cut in pieces[1:]:
        loudness = loudness * one(*cut)
    return loudness


def gaussian(key, shape, scale, limit, shards=(), dtype=jnp.bfloat16):
    values = jax.random.normal(key, shape, jnp.float32) * scale
    if len(shards) > 0:
        values = level_of(key, shape, shards, -0.22, 0.18) * values
    return jnp.clip(values, min=-limit, max=limit).astype(dtype)


def gaussian_with(own_key, extent, deviation, bound, shards, heavy, kind=jnp.bfloat16):
    array = deviation * jax.random.normal(own_key, extent, jnp.float32)
    if shards:
        array = array * level_of(own_key, extent, shards, -0.22, 0.18)
    return jnp.clip(strengthened(array, jax.random.fold_in(own_key, 3), *heavy), -bound, bound).astype(kind)


def setup_inputs(seed: int = 0) -> dict:
    streams_of = jax.random.split(jax.random.key(seed), 15)
    return {
        "section_input": gaussian(streams_of[0], (SECTIONS, L, D), 1.0, 6.0, ((0, 8), (1, 32))),
        "stashed_input": gaussian_with(streams_of[1], (SECTIONS, L, D), 1.0, 6.0, ((0, 8), (1, 32)), (1, 2, 32, 2.75)),
        "output_grad": gaussian(streams_of[2], (SECTIONS, L, D), 1.0, 6.0, ((0, 8), (1, 32))),
        "gain_mixer": jnp.clip(1.0 + 0.18 * jax.random.normal(streams_of[3], (SECTIONS, D), jnp.float32), 0.1, 1.9),
        "gain_channel": jnp.clip(1.0 + 0.18 * jax.random.normal(streams_of[4], (SECTIONS, D), jnp.float32), 0.1, 1.9),
        "factor_first": gaussian(streams_of[5], (SECTIONS, NI, NJ, NJ), NJ ** -0.5, 0.5, ((0, 8), (1, 32))),
        "factor_second": gaussian(streams_of[6], (SECTIONS, NJ, NI, NI), NI ** -0.5, 0.75, ((0, 8), (1, 32))),
        "spectrum": gaussian(streams_of[7], (SECTIONS, NI, NJ, D), 1.0, 6.0, ((0, 8), (2, 32))),
        "factor_third": gaussian(streams_of[8], (SECTIONS, NJ, NI, NI), NI ** -0.5, 0.75, ((0, 8), (1, 32))),
        "factor_fourth": gaussian(streams_of[9], (SECTIONS, NI, NJ, NJ), NJ ** -0.5, 0.5, ((0, 8), (1, 32))),
        "mixer_gate": gaussian(streams_of[10], (SECTIONS, D, D // NB), (D // NB) ** -0.5, 0.375, ((0, 8),)),
        "channel_up": gaussian(streams_of[11], (SECTIONS, D, FF // NB), (D // NB) ** -0.5, 0.375, ((0, 8),)),
        "channel_gate": gaussian(streams_of[12], (SECTIONS, D, FF // NB), (D // NB) ** -0.5, 0.375, ((0, 8),)),
        "channel_down": gaussian(streams_of[13], (SECTIONS, FF, D // NB), (FF // NB) ** -0.5, 0.25, ((0, 8),)),
    }


epsilon = 1e-06

def bround(value):
    return lax.optimization_barrier(value.astype(jnp.bfloat16))

def widened_view(value):
    return value.astype(jnp.float32)

def rms_scale(value_array):
    return lax.rsqrt(lax.optimization_barrier(jnp.mean(value_array * value_array, axis=-1, keepdims=True)) + epsilon)

def norm_back(value_array, scale, gain, incoming_gradient):
    scaled = gain * incoming_gradient
    return scale * scaled - value_array * (scale * scale * scale) * lax.optimization_barrier(jnp.mean(scaled * value_array, axis=-1, keepdims=True))

def block_apply(value_array, weight, block_list):
    item_count = value_array.shape[0]
    reshaped_array = widened_view(weight).reshape(block_list, weight.shape[0] // block_list, weight.shape[1])
    final_output = jnp.einsum('ynq,nqd->ynd', widened_view(value_array).reshape(item_count, block_list, -1), reshaped_array)
    return final_output.reshape(item_count, -1)

def block_back(incoming_gradient, weight, block_list):
    item_count = incoming_gradient.shape[0]
    reshaped_array = widened_view(weight).reshape(block_list, weight.shape[0] // block_list, weight.shape[1])
    final_output = jnp.einsum('eaq,awq->eaw', widened_view(incoming_gradient).reshape(item_count, block_list, -1), reshaped_array)
    return final_output.reshape(item_count, -1)

def block_grad(value_array, incoming_gradient, block_list):
    item_count = value_array.shape[0]
    final_output = jnp.einsum('wli,wld->lid', widened_view(value_array).reshape(item_count, block_list, -1), widened_view(incoming_gradient).reshape(item_count, block_list, -1))
    return final_output.reshape(-1, final_output.shape[2])

def shuffle(value_array, block_list):
    item_count = value_array.shape[0]
    return value_array.reshape(item_count, block_list, block_list, -1).transpose(0, 2, 1, 3).reshape(item_count, -1)

def layer_forward(inputs, gain_one, second_gain, first, second, kernel_here, third, fourth_factor, mixing_weight, up_weight, activation_weight, down_weight):
    wide = widened_view(inputs)
    scale_one = rms_scale(wide)
    normed = bround(wide * scale_one * gain_one)
    folded = bround(jnp.einsum('iqj,ijc->iqc', widened_view(first), widened_view(normed).reshape(NI, NJ, -1)))
    mixed = jnp.einsum('jpi,ijc->pjc', widened_view(second), widened_view(folded))
    filtered = bround(mixed * widened_view(kernel_here))
    returned = bround(jnp.einsum('jpi,ijc->pjc', widened_view(third), widened_view(filtered)))
    back_mixed = jnp.einsum('iqj,ijc->iqc', widened_view(fourth_factor), widened_view(returned)).reshape(NI * NJ, -1)
    gating = block_apply(normed, mixing_weight, NB)
    middle = bround(wide + back_mixed * gating)
    middle_wide = widened_view(middle)
    scale_two = rms_scale(middle_wide)
    normed_two = bround(middle_wide * scale_two * second_gain)
    lifted = block_apply(normed_two, up_weight, NB)
    gated = block_apply(normed_two, activation_weight, NB)
    hidden = bround(jax.nn.silu(gated) * lifted)
    shuffled = shuffle(hidden, NB)
    output = bround(middle_wide + block_apply(shuffled, down_weight, NB))
    saved = (wide, scale_one, normed, mixed, back_mixed, gating, middle_wide, scale_two, normed_two, lifted, gated, shuffled)
    return (output, saved)

def layer_backward(saved, incoming_gradient, gain_one, second_gain, first, second, kernel_here, third, fourth_factor, mixing_weight, up_weight, activation_weight, down_weight):
    wide, scale_one, normed, mixed, back_mixed, gating, middle_wide, scale_two, normed_two, lifted, gated, shuffled = saved
    grad_factor = 1.0 / math.sqrt(NI * NJ)
    up_wide = widened_view(incoming_gradient)
    d_shuffled = bround(block_back(incoming_gradient, down_weight, NB))
    d_hidden = widened_view(shuffle(d_shuffled, NB))
    sigma = jax.nn.sigmoid(gated)
    d_lift = bround(d_hidden * gated * sigma)
    d_gated = bround(d_hidden * lifted * sigma * (1.0 + gated * (1.0 - sigma)))
    d_norm_two = block_back(d_lift, up_weight, NB) + block_back(d_gated, activation_weight, NB)
    d_middle = bround(up_wide + norm_back(middle_wide, scale_two, second_gain, d_norm_two))
    d_mid_wide = widened_view(d_middle)
    d_back = bround(d_mid_wide * gating)
    d_gating = bround(d_mid_wide * back_mixed)
    d_returned = bround(jnp.einsum('iqj,iqc->ijc', widened_view(fourth_factor), widened_view(d_back).reshape(NI, NJ, -1)))
    d_filtered = jnp.einsum('jpi,pjc->ijc', widened_view(third), widened_view(d_returned))
    kernel_grad = (d_filtered * mixed).astype(jnp.bfloat16)
    d_mixed = bround(d_filtered * widened_view(kernel_here))
    d_folded = bround(jnp.einsum('jpi,pjc->ijc', widened_view(second), widened_view(d_mixed)))
    d_normed = jnp.einsum('iqj,iqc->ijc', widened_view(first), widened_view(d_folded)).reshape(NI * NJ, -1)
    d_normed = d_normed + block_back(d_gating, mixing_weight, NB)
    d_input = (d_mid_wide + norm_back(wide, scale_one, gain_one, d_normed)).astype(jnp.bfloat16)
    mix_grad = (block_grad(normed, d_gating, NB) * grad_factor).astype(jnp.bfloat16)
    up_grad = (block_grad(normed_two, d_lift, NB) * grad_factor).astype(jnp.bfloat16)
    act_grad = (block_grad(normed_two, d_gated, NB) * grad_factor).astype(jnp.bfloat16)
    down_grad = (block_grad(shuffled, incoming_gradient, NB) * grad_factor).astype(jnp.bfloat16)
    return (d_input, kernel_grad, mix_grad, up_grad, act_grad, down_grad)

def reference(section_input, stashed_input, output_grad, gain_mixer, gain_channel, factor_first, factor_second, spectrum, factor_third, factor_fourth, mixer_gate, channel_up, channel_gate, channel_down):
    forward_outs = []
    input_grads = []
    kernel_grads = []
    mix_grads = []
    up_grads = []
    act_grads = []
    down_grads = []
    for section in range(N_SECTION):
        weights = (gain_mixer[section], gain_channel[section], factor_first[section], factor_second[section], spectrum[section], factor_third[section], factor_fourth[section], mixer_gate[section], channel_up[section], channel_gate[section], channel_down[section])
        output, unused = layer_forward(section_input[section], *weights)
        forward_outs.append(output)
        recomputed, saved = layer_forward(stashed_input[section], *weights)
        grads = layer_backward(saved, output_grad[section], *weights)
        input_grads.append(grads[0])
        kernel_grads.append(grads[1])
        mix_grads.append(grads[2])
        up_grads.append(grads[3])
        act_grads.append(grads[4])
        down_grads.append(grads[5])
    empty = jnp.zeros((1, NI * NJ, D), jnp.bfloat16)
    next_input = jnp.concatenate([empty, jnp.stack(forward_outs[:-1])], axis=0)
    upstream_grad = jnp.concatenate([jnp.stack(input_grads[1:]), empty], axis=0)
    return (next_input, upstream_grad, jnp.stack(kernel_grads), jnp.stack(mix_grads), jnp.stack(up_grads), jnp.stack(act_grads), jnp.stack(down_grads))
```

```python
import math

import jax
import jax.numpy as jnp
from jax import lax
from jax.experimental import pallas as pl
from jax.experimental.pallas import tpu as pltpu
from jax.sharding import PartitionSpec as P

NB = 4
NI = 64
NJ = 128
D = 1024
FF = 2048
T = 256
HB = FF // NB
DB = D // NB
EPS = 1e-06
KGRAD = 1.0 / math.sqrt(NI * NJ)
GR = 224

F32 = jnp.float32
BF = jnp.bfloat16


def mm(a, b):
    return lax.dot_general(a, b, (((1,), (0,)), ((), ())), preferred_element_type=F32)


def mm_nt(a, b):
    return lax.dot_general(a, b, (((1,), (1,)), ((), ())), preferred_element_type=F32)


def mm_tn(a, b):
    return lax.dot_general(a, b, (((0,), (0,)), ((), ())), preferred_element_type=F32)


def iota(shape, dim):
    return lax.broadcasted_iota(jnp.int32, shape, dim)


def onehot(cond):
    return jnp.where(cond, 1.0, 0.0).astype(BF)


def r_half(r):
    return (r >> 2) & 1


def r_col(r):
    return ((r >> 3) << 2) + (r & 3)


def call(kernel, outs, *args, **kwargs):
    return pl.pallas_call(
        kernel,
        out_shape=[jax.ShapeDtypeStruct(s, d) for s, d in outs],
        compiler_params=pltpu.CompilerParams(vmem_limit_bytes=56 << 20),
        **kwargs,
    )(*args)


def rms(v):
    return lax.rsqrt(jnp.mean(v * v, axis=-1, keepdims=True) + EPS)


def first_rows(first):
    w = first.reshape(T, NJ)
    r, t = iota((T, T), 0), iota((T, T), 1)
    pick = onehot(t == (r_half(r) << 7) + r_col(r))
    return mm(pick, w).astype(BF)


def k_front(x_ref, gain_ref, first_ref, a1_ref):
    rows = first_rows(first_ref[...])
    r, c = iota((T, T), 0), iota((T, T), 1)
    m1 = jnp.where((c >> 7) == r_half(r), jnp.concatenate([rows, rows], axis=1), 0).astype(BF)
    x = x_ref[...].astype(F32)
    n1 = (x * rms(x) * gain_ref[...]).astype(BF)
    a1_ref[...] = mm(m1, n1).astype(BF)


def k_prep(first_ref, second_ref, third_ref, fourth_ref, m1t, m2, m2t, m3, m3t, m4, m4t):
    r, c = iota((T, T), 0), iota((T, T), 1)

    rows = first_rows(first_ref[...])
    e1t = onehot((iota((T, NJ), 0) & 127) == iota((T, NJ), 1))
    m1t[...] = jnp.where((r >> 7) == r_half(c), mm_nt(e1t, rows), 0.0).astype(BF)

    q = onehot(c == ((r & 3) << 6) + (r >> 2))
    e2 = onehot(iota((NI, T), 0) == (iota((NI, T), 1) >> 2))
    e2t = onehot((iota((T, NI), 0) >> 2) == iota((T, NI), 1))
    same = (r & 3) == (c & 3)
    for src, out, out_t in ((second_ref, m2, m2t), (third_ref, m3, m3t)):
        w = mm(q, src[...].reshape(T, NI)).astype(BF)
        out[...] = jnp.where(same, mm(w, e2), 0.0).astype(BF)
        out_t[...] = jnp.where(same, mm_nt(e2t, w), 0.0).astype(BF)

    w4 = fourth_ref[...].reshape(T, NJ)
    e4 = onehot(iota((NJ, T), 0) == r_col(iota((NJ, T), 1)))
    e4t = onehot(r_col(iota((T, NJ), 0)) == iota((T, NJ), 1))
    m4[...] = jnp.where((r >> 7) == r_half(c), mm(w4, e4), 0.0).astype(BF)
    m4t[...] = jnp.where(r_half(r) == (c >> 7), mm_nt(e4t, w4), 0.0).astype(BF)


def k_mid(recv_ref, spec_ref, m2_ref, m3_ref, b1_ref):
    a2 = mm(m2_ref[...], recv_ref[...])
    filt = (a2 * spec_ref[...].astype(F32)).astype(BF)
    b1_ref[...] = mm(m3_ref[...], filt).astype(BF)


def k_mid_keep(recv_ref, spec_ref, m2_ref, m3_ref, b1_ref, a2_ref):
    a2 = mm(m2_ref[...], recv_ref[...])
    a2_ref[...] = a2
    filt = (a2 * spec_ref[...].astype(F32)).astype(BF)
    b1_ref[...] = mm(m3_ref[...], filt).astype(BF)


def k_mid_back(recv_ref, a2_ref, spec_ref, m3t_ref, m2t_ref, da1_ref, sg_ref):
    dfilt = mm(m3t_ref[...], recv_ref[...])
    da2 = (dfilt * spec_ref[...].astype(F32)).astype(BF)
    da1_ref[...] = mm(m2t_ref[...], da2).astype(BF)
    sg_ref[...] = (dfilt * a2_ref[...]).astype(BF)


def cols(b, n):
    return slice(b * n, (b + 1) * n)


def hcols(b, k):
    return slice(k * HB + b * NJ, k * HB + (b + 1) * NJ)


def k_ahead(x_ref, g_ref, gain_ref, mix_ref, down_ref, n1_ref, gate_ref, dhid_ref):
    x = x_ref[...].astype(F32)
    n1_ref[...] = (x * rms(x) * gain_ref[...]).astype(BF)
    for b in range(NB):
        gate_ref[:, cols(b, DB)] = mm(n1_ref[:, cols(b, DB)], mix_ref[cols(b, DB), :])
        dhs = mm_nt(g_ref[:, cols(b, DB)], down_ref[cols(b, HB), :]).astype(BF)
        for k in range(NB):
            dhid_ref[:, hcols(b, k)] = dhs[:, cols(k, NJ)]


def k_tail_back(
    x_ref, recv_ref, g_ref, gate_ref, dhid_ref, m4_ref, m4t_ref, gain_ref, up_ref, act_ref,
    db1_ref, dy1_ref, dgate_ref, n2_ref, hs_ref, dup_ref, dact_ref,
    y1_ref, dn2_ref,
):
    b2 = mm(m4_ref[...], recv_ref[...])
    y1_ref[...] = (x_ref[...].astype(F32) + b2 * gate_ref[...]).astype(BF).astype(F32)
    y1 = y1_ref[...]
    r2 = rms(y1)
    n2_ref[...] = (y1 * r2 * gain_ref[...]).astype(BF)
    for b in range(NB):
        n2 = n2_ref[:, cols(b, DB)]
        up = mm(n2, up_ref[cols(b, DB), :])
        act = mm(n2, act_ref[cols(b, DB), :])
        sg = jax.nn.sigmoid(act)
        silu = act * sg
        hid = (silu * up).astype(BF)
        for k in range(NB):
            hs_ref[:, hcols(b, k)] = hid[:, cols(k, NJ)]
        dhid = dhid_ref[:, cols(b, HB)].astype(F32)
        dup = (dhid * silu).astype(BF)
        dact = (dhid * up * sg * (1.0 + act * (1.0 - sg))).astype(BF)
        dup_ref[:, cols(b, HB)] = dup
        dact_ref[:, cols(b, HB)] = dact
        dn2_ref[:, cols(b, DB)] = mm_nt(dup, up_ref[cols(b, DB), :]) + mm_nt(
            dact, act_ref[cols(b, DB), :]
        )
    s = gain_ref[...] * dn2_ref[...]
    y1 = y1_ref[...]
    back = r2 * s - y1 * (r2 * r2 * r2) * jnp.mean(s * y1, axis=-1, keepdims=True)
    dy1 = (g_ref[...].astype(F32) + back).astype(BF)
    dy1_ref[...] = dy1
    dyw = dy1.astype(F32)
    db2 = (dyw * gate_ref[...]).astype(BF)
    db1_ref[...] = mm(m4t_ref[...], db2).astype(BF)
    dgate_ref[...] = (dyw * mm(m4_ref[...], recv_ref[...])).astype(BF)


def k_grads(n1_ref, dgate_ref, n2_ref, dup_ref, dact_ref, hs_ref, g_ref, mix_ref, o_ref, dn1_ref):
    for b in range(NB):
        d = slice(8 * b, 8 * b + 8)
        dgate = dgate_ref[:, cols(b, DB)]
        dn1_ref[:, cols(b, DB)] = mm_nt(dgate, mix_ref[cols(b, DB), :])
        mix = mm_tn(n1_ref[:, cols(b, DB)], dgate) * KGRAD
        o_ref[d, 0:32, :] = mix.astype(BF).reshape(8, 32, DB)
        n2 = n2_ref[:, cols(b, DB)]
        up = (mm_tn(n2, dup_ref[:, cols(b, HB)]) * KGRAD).astype(BF).reshape(8, 32, HB)
        o_ref[d, 32:64, :] = up[:, :, :DB]
        o_ref[d, 64:96, :] = up[:, :, DB:]
        act = (mm_tn(n2, dact_ref[:, cols(b, HB)]) * KGRAD).astype(BF).reshape(8, 32, HB)
        o_ref[d, 96:128, :] = act[:, :, :DB]
        o_ref[d, 128:160, :] = act[:, :, DB:]
        down = mm_tn(hs_ref[:, cols(b, HB)], g_ref[:, cols(b, DB)]) * KGRAD
        o_ref[d, 160:224, :] = down.astype(BF).reshape(8, 64, DB)


def k_tail(x_ref, recv_ref, m4_ref, gain1_ref, gain2_ref, mix_ref, up_ref, act_ref, down_ref,
           out_ref, y1_ref, n_ref, hs_ref):
    x = x_ref[...].astype(F32)
    n_ref[...] = (x * rms(x) * gain1_ref[...]).astype(BF)
    b2 = mm(m4_ref[...], recv_ref[...])
    for b in range(NB):
        gate = mm(n_ref[:, cols(b, DB)], mix_ref[cols(b, DB), :])
        y1_ref[:, cols(b, DB)] = (
            (x_ref[:, cols(b, DB)].astype(F32) + b2[:, cols(b, DB)] * gate).astype(BF).astype(F32)
        )
    y1 = y1_ref[...]
    n_ref[...] = (y1 * rms(y1) * gain2_ref[...]).astype(BF)
    for b in range(NB):
        n2 = n_ref[:, cols(b, DB)]
        up = mm(n2, up_ref[cols(b, DB), :])
        act = mm(n2, act_ref[cols(b, DB), :])
        hid = (act * jax.nn.sigmoid(act) * up).astype(BF)
        for k in range(NB):
            hs_ref[:, hcols(b, k)] = hid[:, cols(k, NJ)]
    for b in range(NB):
        out_ref[:, cols(b, DB)] = (
            y1_ref[:, cols(b, DB)] + mm(hs_ref[:, cols(b, HB)], down_ref[cols(b, HB), :])
        ).astype(BF)


def k_end(x_ref, recv_ref, m1t_ref, dn1_ref, dy1_ref, gain_ref, dx_ref):
    x = x_ref[...].astype(F32)
    r1 = rms(x)
    s = gain_ref[...] * (mm(m1t_ref[...], recv_ref[...]) + dn1_ref[...])
    back = r1 * s - x * (r1 * r1 * r1) * jnp.mean(s * x, axis=-1, keepdims=True)
    dx_ref[...] = (dy1_ref[...].astype(F32) + back).astype(BF)


def k_sum(recv_ref, mix_ref, up_ref, act_ref, down_ref):
    total = recv_ref[0].astype(F32)
    for s in range(1, recv_ref.shape[0]):
        total = total + recv_ref[s].astype(F32)
    total = total.astype(BF)
    mix_ref[...] = total[0:32]
    up_ref[:, :DB] = total[32:64]
    up_ref[:, DB:] = total[64:96]
    act_ref[:, :DB] = total[96:128]
    act_ref[:, DB:] = total[128:160]
    down_ref[...] = total[160:224]


def swap(v):
    return lax.all_to_all(v, "seq", split_axis=0, concat_axis=0, tiled=True)


def shift(v, by):
    n = lax.axis_size("section")
    return lax.ppermute(v, "section", [(i, i + by) for i in range(n) if 0 <= i + by < n])


def shards(xa, xb, g, gain1, gain2, first, second, spec, third, fourth, mix, up, act, down):
    xa, xb, g = xa[0], xb[0], g[0]
    first, second, third, fourth = first[0], second[0], third[0], fourth[0]
    mix, up, act, down = mix[0], up[0], act[0], down[0]
    spec = spec[0].reshape(T, D)
    td, tt = (T, D), (T, T)

    (a1b,) = call(k_front, [(td, BF)], xb, gain1, first)
    rb = swap(a1b)
    (a1a,) = call(k_front, [(td, BF)], xa, gain1, first)
    ra = swap(a1a)
    m1t, m2, m2t, m3, m3t, m4, m4t = call(k_prep, [(tt, BF)] * 7, first, second, third, fourth)
    n1b, gateb, dhid = call(
        k_ahead, [(td, BF), (td, F32), ((T, FF), BF)], xb, g, gain1, mix, down
    )
    b1b, a2b = call(k_mid_keep, [(td, BF), (td, F32)], rb, spec, m2, m3)
    qb = swap(b1b)
    (b1a,) = call(k_mid, [(td, BF)], ra, spec, m2, m3)
    qa = swap(b1a)
    db1, dy1, dgate, n2, hs, dup, dact = call(
        k_tail_back,
        [(td, BF)] * 4 + [((T, FF), BF)] * 3,
        xb, qb, g, gateb, dhid, m4, m4t, gain2, up, act,
        scratch_shapes=[pltpu.VMEM(td, F32), pltpu.VMEM(td, F32)],
    )
    rc = swap(db1)
    grads, dn1 = call(
        k_grads, [((32, GR, DB), BF), (td, F32)], n1b, dgate, n2, dup, dact, hs, g, mix
    )
    gr = swap(grads)
    (outa,) = call(
        k_tail, [(td, BF)], xa, qa, m4, gain1, gain2, mix, up, act, down,
        scratch_shapes=[pltpu.VMEM(td, F32), pltpu.VMEM(td, BF), pltpu.VMEM((T, FF), BF)],
    )
    next_input = shift(outa, 1)
    da1, sgrad = call(k_mid_back, [(td, BF), (td, BF)], rc, a2b, spec, m3t, m2t)
    rd = swap(da1)
    (dx,) = call(k_end, [(td, BF)], xb, rd, m1t, dn1, dy1, gain1)
    upstream = shift(dx, -1)
    gm, gu, ga, gd = call(
        k_sum,
        [((32, DB), BF), ((32, HB), BF), ((32, HB), BF), ((64, DB), BF)],
        gr,
    )
    return (
        next_input[None],
        upstream[None],
        sgrad.reshape(1, NI, 4, D),
        gm[None],
        gu[None],
        ga[None],
        gd[None],
    )


def solution(mesh):
    in_specs = (
        P("section", "seq", None),
        P("section", "seq", None),
        P("section", "seq", None),
        P("section", None),
        P("section", None),
        P("section", "seq", None, None),
        P("section", "seq", None, None),
        P("section", None, "seq", None),
        P("section", "seq", None, None),
        P("section", "seq", None, None),
        P("section", None, None),
        P("section", None, None),
        P("section", None, None),
        P("section", None, None),
    )
    out_specs = (
        P("section", "seq", None),
        P("section", "seq", None),
        P("section", None, "seq", None),
        P("section", "seq", None),
        P("section", "seq", None),
        P("section", "seq", None),
        P("section", "seq", None),
    )
    return jax.shard_map(shards, mesh=mesh, in_specs=in_specs, out_specs=out_specs, check_vma=False)
```

```python
import math

import jax
import jax.numpy as jnp
from jax import lax
from jax.experimental import pallas as pl
from jax.experimental.pallas import tpu as pltpu
from jax.sharding import PartitionSpec as P

NB = 4
NI = 64
NJ = 128
D = 1024
FF = 2048
T = 256
HB = FF // NB
DB = D // NB
EPS = 1e-06
KGRAD = 1.0 / math.sqrt(NI * NJ)
GR = 224

F32 = jnp.float32
BF = jnp.bfloat16


def mm(a, b):
    return lax.dot_general(a, b, (((1,), (0,)), ((), ())), preferred_element_type=F32)


def mm_nt(a, b):
    return lax.dot_general(a, b, (((1,), (1,)), ((), ())), preferred_element_type=F32)


def mm_tn(a, b):
    return lax.dot_general(a, b, (((0,), (0,)), ((), ())), preferred_element_type=F32)


def iota(shape, dim):
    return lax.broadcasted_iota(jnp.int32, shape, dim)


def onehot(cond):
    return jnp.where(cond, 1.0, 0.0).astype(BF)


def r_half(r):
    return (r >> 2) & 1


def r_col(r):
    return ((r >> 3) << 2) + (r & 3)


class Lazy:
    def __init__(self, copy, ref):
        self.copy, self.ref, self.waited = copy, ref, False

    def get(self):
        if not self.waited:
            self.copy.wait()
            self.waited = True
        return self.ref

    def __getitem__(self, index):
        return self.get()[index]


class Late:
    def __init__(self, copy, ref):
        self.copy, self.ref, self.flushed = copy, ref, False

    def __getitem__(self, index):
        return self.ref[index]

    def __setitem__(self, index, value):
        self.ref[index] = value

    def flush(self):
        self.copy.start()
        self.flushed = True


def call(kernel, outs, *args, scratch=(), mib=40):
    arrays = [a for a, _ in args]
    in_roles, out_roles = [r for _, r in args], [o[2] for o in outs]
    n_in, n_out = len(args), len(outs)
    ins_h = [i for i, r in enumerate(in_roles) if r == "h"]
    outs_h = [i for i, r in enumerate(out_roles) if r == "h"]
    spec = {"v": pl.BlockSpec(memory_space=pltpu.VMEM), "h": pl.BlockSpec(memory_space=pltpu.HBM)}
    bufs = [pltpu.VMEM(arrays[i].shape, arrays[i].dtype) for i in ins_h]
    bufs += [pltpu.VMEM(outs[i][0], outs[i][1]) for i in outs_h]
    n_buf = len(bufs)

    def body(*refs):
        ins, results = list(refs[:n_in]), list(refs[n_in : n_in + n_out])
        vmem = refs[n_in + n_out : n_in + n_out + n_buf]
        sems = refs[n_in + n_out + n_buf]
        rest = refs[n_in + n_out + n_buf + 1 :]
        for k, i in enumerate(ins_h):
            copy = pltpu.make_async_copy(ins[i], vmem[k], sems.at[k])
            copy.start()
            ins[i] = Lazy(copy, vmem[k])
        for k, i in enumerate(outs_h, len(ins_h)):
            results[i] = Late(pltpu.make_async_copy(vmem[k], results[i], sems.at[k]), vmem[k])
        kernel(*ins, *results, *rest)
        for i in ins_h:
            ins[i].get()
        for i in outs_h:
            if not results[i].flushed:
                results[i].flush()
        for i in outs_h:
            results[i].copy.wait()

    return pl.pallas_call(
        body,
        out_shape=[
            (pltpu.HBM if o[2] == "h" else jax.ShapeDtypeStruct)(o[0], o[1]) for o in outs
        ],
        in_specs=[spec[r] for r in in_roles],
        out_specs=[spec[r] for r in out_roles],
        scratch_shapes=bufs + [pltpu.SemaphoreType.DMA((max(n_buf, 1),))] + list(scratch),
        compiler_params=pltpu.CompilerParams(vmem_limit_bytes=mib << 20),
    )(*(pltpu.with_memory_space_constraint(a, pltpu.HBM) if r == "h" else a for a, r in args))


def rms(v):
    return lax.rsqrt(jnp.mean(v * v, axis=-1, keepdims=True) + EPS)


def first_rows(first):
    w = first.reshape(T, NJ)
    r, t = iota((T, T), 0), iota((T, T), 1)
    pick = onehot(t == (r_half(r) << 7) + r_col(r))
    return mm(pick, w).astype(BF)


def k_front(first_ref, x_ref, gain_ref, a1_ref):
    rows = first_rows(first_ref[...])
    r, c = iota((T, T), 0), iota((T, T), 1)
    m1 = jnp.where((c >> 7) == r_half(r), jnp.concatenate([rows, rows], axis=1), 0).astype(BF)
    x = x_ref[...].astype(F32)
    n1 = (x * rms(x) * gain_ref[...]).astype(BF)
    a1_ref[...] = mm(m1, n1).astype(BF)


def k_prep(first_ref, second_ref, third_ref, fourth_ref, m1t, m2, m2t, m3, m3t, m4, m4t):
    r, c = iota((T, T), 0), iota((T, T), 1)

    rows = first_rows(first_ref[...])
    e1t = onehot((iota((T, NJ), 0) & 127) == iota((T, NJ), 1))
    m1t[...] = jnp.where((r >> 7) == r_half(c), mm_nt(e1t, rows), 0.0).astype(BF)

    q = onehot(c == ((r & 3) << 6) + (r >> 2))
    e2 = onehot(iota((NI, T), 0) == (iota((NI, T), 1) >> 2))
    e2t = onehot((iota((T, NI), 0) >> 2) == iota((T, NI), 1))
    same = (r & 3) == (c & 3)
    for src, out, out_t in ((second_ref, m2, m2t), (third_ref, m3, m3t)):
        w = mm(q, src[...].reshape(T, NI)).astype(BF)
        out[...] = jnp.where(same, mm(w, e2), 0.0).astype(BF)
        out_t[...] = jnp.where(same, mm_nt(e2t, w), 0.0).astype(BF)

    w4 = fourth_ref[...].reshape(T, NJ)
    e4 = onehot(iota((NJ, T), 0) == r_col(iota((NJ, T), 1)))
    e4t = onehot(r_col(iota((T, NJ), 0)) == iota((T, NJ), 1))
    m4[...] = jnp.where((r >> 7) == r_half(c), mm(w4, e4), 0.0).astype(BF)
    m4t[...] = jnp.where(r_half(r) == (c >> 7), mm_nt(e4t, w4), 0.0).astype(BF)


def k_mid(recv_ref, m2_ref, spec_ref, m3_ref, a1_ref, send_ref, a2_ref):
    a2 = mm(m2_ref[...], recv_ref[...])
    a2_ref[...] = a2
    a2_ref.flush()
    filt = (a2 * spec_ref[...].astype(F32)).astype(BF)
    send_ref[:, :D] = mm(m3_ref[...], filt).astype(BF)
    send_ref[:, D:] = a1_ref[...]


def k_mid_back(recv_ref, m3t_ref, a2_ref, spec_ref, m2t_ref, da1_ref, sg_ref):
    dfilt = mm(m3t_ref[...], recv_ref[:, :D])
    sg_ref[...] = (dfilt * a2_ref[...]).astype(BF)
    sg_ref.flush()
    da2 = (dfilt * spec_ref[...].astype(F32)).astype(BF)
    da1_ref[...] = mm(m2t_ref[...], da2).astype(BF)


def cols(b, n):
    return slice(b * n, (b + 1) * n)


def hcols(b, k):
    return slice(k * HB + b * NJ, k * HB + (b + 1) * NJ)


def k_ahead(x_ref, gain_ref, mix_ref, g_ref, down_ref, n1_ref, gate_ref, dhid_ref):
    x = x_ref[...].astype(F32)
    n1_ref[...] = (x * rms(x) * gain_ref[...]).astype(BF)
    for b in range(NB):
        gate_ref[:, cols(b, DB)] = mm(n1_ref[:, cols(b, DB)], mix_ref[cols(b, DB), :])
        dhs = mm_nt(g_ref[:, cols(b, DB)], down_ref[cols(b, HB), :]).astype(BF)
        for k in range(NB):
            dhid_ref[:, hcols(b, k)] = dhs[:, cols(k, NJ)]


def k_tail_back(
    recv_ref, m4_ref, x_ref, gate_ref, gain_ref, up_ref, act_ref, dhid_ref, g_ref, m4t_ref,
    m2_ref, spec_ref, m3_ref,
    send_ref, dy1_ref, dgate_ref, n2_ref, hs_ref, dup_ref, dact_ref,
    y1_ref, dn2_ref, b2_ref,
):
    b2_ref[...] = mm(m4_ref[...], recv_ref[:, :D])
    y1_ref[...] = (x_ref[...].astype(F32) + b2_ref[...] * gate_ref[...]).astype(BF).astype(F32)
    y1 = y1_ref[...]
    r2 = rms(y1)
    n2_ref[...] = (y1 * r2 * gain_ref[...]).astype(BF)
    n2_ref.flush()
    for b in range(NB):
        n2 = n2_ref[:, cols(b, DB)]
        up = mm(n2, up_ref[cols(b, DB), :])
        act = mm(n2, act_ref[cols(b, DB), :])
        sg = jax.nn.sigmoid(act)
        silu = act * sg
        hid = (silu * up).astype(BF)
        for k in range(NB):
            hs_ref[:, hcols(b, k)] = hid[:, cols(k, NJ)]
        dhid = dhid_ref[:, cols(b, HB)].astype(F32)
        dup = (dhid * silu).astype(BF)
        dact = (dhid * up * sg * (1.0 + act * (1.0 - sg))).astype(BF)
        dup_ref[:, cols(b, HB)] = dup
        dact_ref[:, cols(b, HB)] = dact
        dn2_ref[:, cols(b, DB)] = mm_nt(dup, up_ref[cols(b, DB), :]) + mm_nt(
            dact, act_ref[cols(b, DB), :]
        )
    hs_ref.flush()
    dup_ref.flush()
    dact_ref.flush()
    s = gain_ref[...] * dn2_ref[...]
    y1 = y1_ref[...]
    back = r2 * s - y1 * (r2 * r2 * r2) * jnp.mean(s * y1, axis=-1, keepdims=True)
    dy1 = (g_ref[...].astype(F32) + back).astype(BF)
    dy1_ref[...] = dy1
    dy1_ref.flush()
    dyw = dy1.astype(F32)
    dgate_ref[...] = (dyw * b2_ref[...]).astype(BF)
    dgate_ref.flush()
    db2 = (dyw * gate_ref[...]).astype(BF)
    send_ref[:, :D] = mm(m4t_ref[...], db2).astype(BF)
    filt = (mm(m2_ref[...], recv_ref[:, D:]) * spec_ref[...].astype(F32)).astype(BF)
    send_ref[:, D:] = mm(m3_ref[...], filt).astype(BF)


def k_grads(
    n1_ref, dgate_ref, mix_ref, n2_ref, dup_ref, dact_ref, hs_ref, g_ref,
    keep_ref, send_ref, dn1_ref,
):
    core = lax.axis_index("seq")

    def put(b, rows, value):
        v = (value * KGRAD).astype(BF).reshape(4, 2, rows.stop - rows.start, DB)

        @pl.when((core & 1) == 0)
        def _():
            keep_ref[b, :, rows, :] = v[:, 0]
            send_ref[b, :, rows, :] = v[:, 1]

        @pl.when((core & 1) == 1)
        def _():
            keep_ref[b, :, rows, :] = v[:, 1]
            send_ref[b, :, rows, :] = v[:, 0]

    for b in range(NB):
        dgate = dgate_ref[:, cols(b, DB)]
        dn1_ref[:, cols(b, DB)] = mm_nt(dgate, mix_ref[cols(b, DB), :])
        put(b, slice(0, 32), mm_tn(n1_ref[:, cols(b, DB)], dgate))
        n2 = n2_ref[:, cols(b, DB)]
        for h in range(2):
            put(b, slice(32 + 32 * h, 64 + 32 * h), mm_tn(n2, dup_ref[:, cols(2 * b + h, DB)]))
            put(b, slice(96 + 32 * h, 128 + 32 * h), mm_tn(n2, dact_ref[:, cols(2 * b + h, DB)]))
        put(b, slice(160, 224), mm_tn(hs_ref[:, cols(b, HB)], g_ref[:, cols(b, DB)]))


def k_sum_core(keep_ref, recv_ref, *outs):
    for dy in range(4):
        y = ((lax.axis_index("seq") >> 1) + dy) & 3
        for x in range(4):
            outs[dy][x] = (keep_ref[x, y].astype(F32) + recv_ref[x, y].astype(F32)).astype(BF)
        outs[dy].flush()


def k_sum_y(a_ref, b_ref, c_ref, d_ref, *outs):
    for dx in range(4):
        x = ((lax.axis_index("seq") >> 3) + dx) & 3
        outs[dx][...] = (
            a_ref[x].astype(F32) + b_ref[x].astype(F32) + c_ref[x].astype(F32) + d_ref[x].astype(F32)
        ).astype(BF)


def k_sum_x(a_ref, b_ref, c_ref, d_ref, mix_ref, up_ref, act_ref, down_ref):
    def total(r):
        return (
            a_ref[r].astype(F32) + b_ref[r].astype(F32) + c_ref[r].astype(F32) + d_ref[r].astype(F32)
        ).astype(BF)

    mix_ref[...] = total(slice(0, 32))
    up_ref[:, :DB] = total(slice(32, 64))
    up_ref[:, DB:] = total(slice(64, 96))
    act_ref[:, :DB] = total(slice(96, 128))
    act_ref[:, DB:] = total(slice(128, 160))
    down_ref[...] = total(slice(160, 224))


def k_tail(recv_ref, m4_ref, x_ref, gain1_ref, mix_ref, gain2_ref, up_ref, act_ref, down_ref,
           out_ref, y1_ref, n_ref, hs_ref):
    x = x_ref[...].astype(F32)
    n_ref[...] = (x * rms(x) * gain1_ref[...]).astype(BF)
    b2 = mm(m4_ref[...], recv_ref[:, D:])
    for b in range(NB):
        gate = mm(n_ref[:, cols(b, DB)], mix_ref[cols(b, DB), :])
        y1_ref[:, cols(b, DB)] = (
            (x_ref[:, cols(b, DB)].astype(F32) + b2[:, cols(b, DB)] * gate).astype(BF).astype(F32)
        )
    y1 = y1_ref[...]
    n_ref[...] = (y1 * rms(y1) * gain2_ref[...]).astype(BF)
    for b in range(NB):
        n2 = n_ref[:, cols(b, DB)]
        up = mm(n2, up_ref[cols(b, DB), :])
        act = mm(n2, act_ref[cols(b, DB), :])
        hid = (act * jax.nn.sigmoid(act) * up).astype(BF)
        for k in range(NB):
            hs_ref[:, hcols(b, k)] = hid[:, cols(k, NJ)]
    for b in range(NB):
        out_ref[:, cols(b, DB)] = (
            y1_ref[:, cols(b, DB)] + mm(hs_ref[:, cols(b, HB)], down_ref[cols(b, HB), :])
        ).astype(BF)


def k_end(recv_ref, m1t_ref, x_ref, gain_ref, dn1_ref, dy1_ref, dx_ref):
    x = x_ref[...].astype(F32)
    r1 = rms(x)
    s = gain_ref[...] * (mm(m1t_ref[...], recv_ref[...]) + dn1_ref[...])
    back = r1 * s - x * (r1 * r1 * r1) * jnp.mean(s * x, axis=-1, keepdims=True)
    dx_ref[...] = (dy1_ref[...].astype(F32) + back).astype(BF)


def swap(v):
    return lax.all_to_all(v, "seq", split_axis=0, concat_axis=0, tiled=True)


def ring_y(d):
    return [(i, (i & 25) + ((((i >> 1) + d) & 3) << 1)) for i in range(32)]


def ring_x(d):
    return [(i, (i + 8 * d) & 31) for i in range(32)]


def shift(v, by):
    n = lax.axis_size("section")
    return lax.ppermute(v, "section", [(i, i + by) for i in range(n) if 0 <= i + by < n])


def shards(xa, xb, g, gain1, gain2, first, second, spec, third, fourth, mix, up, act, down):
    xa, xb, g = xa[0], xb[0], g[0]
    first, second, third, fourth = first[0], second[0], third[0], fourth[0]
    mix, up, act, down = mix[0], up[0], act[0], down[0]
    spec = spec[0].reshape(T, D)

    return body(xa, xb, g, gain1, gain2, first, second, spec, third, fourth, mix, up, act, down)


def h(*arrays):
    return [(a, "h") for a in arrays]


def v(*arrays):
    return [(a, "v") for a in arrays]


def body(xa, xb, g, gain1, gain2, first, second, spec, third, fourth, mix, up, act, down):
    td, tt = (T, D), (T, T)
    (a1b,) = call(k_front, [(td, BF, "v")], *h(first, xb, gain1))
    r1 = swap(a1b)
    (a1a,) = call(k_front, [(td, BF, "h")], *h(first, xa, gain1))
    m1t, m2, m2t, m3, m3t, m4, m4t = call(
        k_prep, [(tt, BF, "h")] * 7, *h(first, second, third, fourth)
    )
    send2, a2b = call(k_mid, [((T, 2 * D), BF, "v"), (td, F32, "h")], *v(r1), *h(m2, spec, m3, a1a))
    r2 = swap(send2)
    n1b, gateb, dhid = call(
        k_ahead,
        [(td, BF, "h"), (td, F32, "h"), ((T, FF), BF, "h")],
        *h(xb, gain1, mix, g, down),
    )
    send3, dy1, dgate, n2, hs, dup, dact = call(
        k_tail_back,
        [((T, 2 * D), BF, "v")] + [(td, BF, "h")] * 3 + [((T, FF), BF, "h")] * 3,
        *v(r2),
        *h(m4, xb, gateb, gain2, up, act, dhid, g, m4t, m2, spec, m3),
        scratch=[pltpu.VMEM(td, F32)] * 3,
    )
    r3 = swap(send3)
    keep, other, dn1 = call(
        k_grads,
        [((4, 4, GR, DB), BF, "h"), ((4, 4, GR, DB), BF, "h"), (td, F32, "h")],
        *h(n1b, dgate, mix, n2, dup, dact, hs, g),
    )
    other = lax.ppermute(other, "seq", [(i, i ^ 1) for i in range(32)])
    s0, *sy = call(k_sum_core, [((4, GR, DB), BF, "h")] * 4, *h(keep, other))
    sy = [lax.ppermute(p, "seq", ring_y(d + 1)) for d, p in enumerate(sy)]
    da1, sgrad = call(k_mid_back, [(td, BF, "v"), (td, BF, "h")], *v(r3), *h(m3t, a2b, spec, m2t))
    r4 = swap(da1)
    (outa,) = call(
        k_tail, [(td, BF, "h")], *h(r3, m4, xa, gain1, mix, gain2, up, act, down),
        scratch=[pltpu.VMEM(td, F32), pltpu.VMEM(td, BF), pltpu.VMEM((T, FF), BF)],
    )
    next_input = shift(outa, 1)
    (dx,) = call(k_end, [(td, BF, "h")], *v(r4), *h(m1t, xb, gain1, dn1, dy1))
    upstream = shift(dx, -1)
    s0, *sx = call(k_sum_y, [((GR, DB), BF, "h")] * 4, *h(s0, *sy))
    sx = [lax.ppermute(p, "seq", ring_x(d + 1)) for d, p in enumerate(sx)]
    gm, gu, ga, gd = call(
        k_sum_x,
        [((32, DB), BF, "h"), ((32, HB), BF, "h"), ((32, HB), BF, "h"), ((64, DB), BF, "h")],
        *h(s0, *sx),
    )
    return (
        next_input[None],
        upstream[None],
        sgrad.reshape(1, NI, 4, D),
        gm[None],
        gu[None],
        ga[None],
        gd[None],
    )


def solution(mesh):
    in_specs = (
        P("section", "seq", None),
        P("section", "seq", None),
        P("section", "seq", None),
        P("section", None),
        P("section", None),
        P("section", "seq", None, None),
        P("section", "seq", None, None),
        P("section", None, "seq", None),
        P("section", "seq", None, None),
        P("section", "seq", None, None),
        P("section", None, None),
        P("section", None, None),
        P("section", None, None),
        P("section", None, None),
    )
    out_specs = (
        P("section", "seq", None),
        P("section", "seq", None),
        P("section", None, "seq", None),
        P("section", "seq", None),
        P("section", "seq", None),
        P("section", "seq", None),
        P("section", "seq", None),
    )
    return jax.shard_map(shards, mesh=mesh, in_specs=in_specs, out_specs=out_specs, check_vma=False)
```

```python
import math

import jax
import jax.numpy as jnp
from jax import lax
from jax.experimental import pallas as pl
from jax.experimental.pallas import tpu as pltpu
from jax.sharding import PartitionSpec as P

NB = 4
NI = 64
NJ = 128
D = 1024
FF = 2048
T = 256
HB = FF // NB
DB = D // NB
EPS = 1e-06
KGRAD = 1.0 / math.sqrt(NI * NJ)
GR = 224

F32 = jnp.float32
BF = jnp.bfloat16


def mm(a, b):
    return lax.dot_general(a, b, (((1,), (0,)), ((), ())), preferred_element_type=F32)


def mm_nt(a, b):
    return lax.dot_general(a, b, (((1,), (1,)), ((), ())), preferred_element_type=F32)


def iota(shape, dim):
    return lax.broadcasted_iota(jnp.int32, shape, dim)


def onehot(cond):
    return jnp.where(cond, 1.0, 0.0).astype(BF)


def r_half(r):
    return (r >> 2) & 1


def r_col(r):
    return ((r >> 3) << 2) + (r & 3)


class Lazy:
    def __init__(self, copies, ref):
        self.copies, self.ref, self.waited = copies, ref, set()

    def get(self, part=None):
        for k in range(len(self.copies)) if part is None else (part,):
            if k not in self.waited:
                self.copies[k].wait()
                self.waited.add(k)
        return self.ref

    def __getitem__(self, index):
        return self.get()[index]


class Late:
    def __init__(self, copies, ref):
        self.copies, self.ref, self.started = copies, ref, set()

    def __getitem__(self, index):
        return self.ref[index]

    def __setitem__(self, index, value):
        self.ref[index] = value

    def flush(self, part=None):
        for k in range(len(self.copies)) if part is None else (part,):
            if k not in self.started:
                self.copies[k].start()
                self.started.add(k)


PARTS = {"h": None, "x": 0, "c": 1}


def cuts(src, dst, sems, at, role, shape):
    if role == "h":
        return [pltpu.make_async_copy(src, dst, sems.at[at])]
    n = shape[PARTS[role]] // 4
    parts = [(slice(None),) * PARTS[role] + (pl.ds(k * n, n),) for k in range(4)]
    return [
        pltpu.make_async_copy(src.at[p], dst.at[p], sems.at[at + k]) for k, p in enumerate(parts)
    ]


def call(kernel, outs, *args, scratch=(), mib=40):
    arrays = [a for a, _ in args]
    in_roles, out_roles = [r for _, r in args], [o[2] for o in outs]
    n_in, n_out = len(args), len(outs)
    ins_h = [i for i, r in enumerate(in_roles) if r in PARTS]
    outs_h = [i for i, r in enumerate(out_roles) if r in PARTS]
    vm, hb = pl.BlockSpec(memory_space=pltpu.VMEM), pl.BlockSpec(memory_space=pltpu.HBM)
    bufs = [pltpu.VMEM(arrays[i].shape, arrays[i].dtype) for i in ins_h]
    bufs += [pltpu.VMEM(outs[i][0], outs[i][1]) for i in outs_h]
    n_buf = len(bufs)

    def body(*refs):
        ins, results = list(refs[:n_in]), list(refs[n_in : n_in + n_out])
        vmem = refs[n_in + n_out : n_in + n_out + n_buf]
        sems = refs[n_in + n_out + n_buf]
        rest = refs[n_in + n_out + n_buf + 1 :]
        at = 0
        for k, i in enumerate(ins_h):
            ins[i] = Lazy(cuts(ins[i], vmem[k], sems, at, in_roles[i], arrays[i].shape), vmem[k])
            for copy in ins[i].copies:
                copy.start()
            at += 4
        for k, i in enumerate(outs_h, len(ins_h)):
            copies = cuts(vmem[k], results[i], sems, at, out_roles[i], outs[i][0])
            results[i] = Late(copies, vmem[k])
            at += 4
        kernel(*ins, *results, *rest)
        for i in ins_h:
            ins[i].get()
        for i in outs_h:
            results[i].flush()
        for i in outs_h:
            for copy in results[i].copies:
                copy.wait()

    return pl.pallas_call(
        body,
        out_shape=[
            (jax.ShapeDtypeStruct if o[2] == "v" else pltpu.HBM)(o[0], o[1]) for o in outs
        ],
        in_specs=[vm if r == "v" else hb for r in in_roles],
        out_specs=[vm if r == "v" else hb for r in out_roles],
        scratch_shapes=bufs + [pltpu.SemaphoreType.DMA((4 * max(n_buf, 1),))] + list(scratch),
        compiler_params=pltpu.CompilerParams(vmem_limit_bytes=mib << 20),
    )(*(a if r == "v" else pltpu.with_memory_space_constraint(a, pltpu.HBM) for a, r in args))


def rows_of(n):
    return [slice(r, r + n) for r in range(0, T, n)]


def rms(v):
    return lax.rsqrt(jnp.mean(v * v, axis=-1, keepdims=True) + EPS)


def first_rows(first):
    w = first.reshape(T, NJ)
    r, t = iota((T, T), 0), iota((T, T), 1)
    pick = onehot(t == (r_half(r) << 7) + r_col(r))
    return mm(pick, w).astype(BF)


def k_front(first_ref, x_ref, gain_ref, a1_ref, n1_ref):
    rows = first_rows(first_ref[...])
    r, c = iota((T, T), 0), iota((T, T), 1)
    m1 = jnp.where((c >> 7) == r_half(r), jnp.concatenate([rows, rows], axis=1), 0).astype(BF)
    gain = gain_ref[...]
    for k in range(4):
        x_ref.get(k)
        for q in rows_of(16)[4 * k : 4 * k + 4]:
            x = x_ref.ref[q, :].astype(F32)
            n1_ref[q, :] = (x * rms(x) * gain).astype(BF)
    for k in range(4):
        a1_ref[:, cols(k, DB)] = mm(m1, n1_ref[:, cols(k, DB)]).astype(BF)
        a1_ref.flush(k)


def k_prep(first_ref, second_ref, third_ref, fourth_ref, m1t, m2, m2t, m3, m3t, m4, m4t):
    r, c = iota((T, T), 0), iota((T, T), 1)

    rows = first_rows(first_ref[...])
    e1t = onehot((iota((T, NJ), 0) & 127) == iota((T, NJ), 1))
    m1t[...] = jnp.where((r >> 7) == r_half(c), mm_nt(e1t, rows), 0.0).astype(BF)

    q = onehot(c == ((r & 3) << 6) + (r >> 2))
    e2 = onehot(iota((NI, T), 0) == (iota((NI, T), 1) >> 2))
    e2t = onehot((iota((T, NI), 0) >> 2) == iota((T, NI), 1))
    same = (r & 3) == (c & 3)
    for src, out, out_t in ((second_ref, m2, m2t), (third_ref, m3, m3t)):
        w = mm(q, src[...].reshape(T, NI)).astype(BF)
        out[...] = jnp.where(same, mm(w, e2), 0.0).astype(BF)
        out_t[...] = jnp.where(same, mm_nt(e2t, w), 0.0).astype(BF)

    w4 = fourth_ref[...].reshape(T, NJ)
    e4 = onehot(iota((NJ, T), 0) == r_col(iota((NJ, T), 1)))
    e4t = onehot(r_col(iota((T, NJ), 0)) == iota((T, NJ), 1))
    m4[...] = jnp.where((r >> 7) == r_half(c), mm(w4, e4), 0.0).astype(BF)
    m4t[...] = jnp.where(r_half(r) == (c >> 7), mm_nt(e4t, w4), 0.0).astype(BF)


def k_mid(recv_ref, m2_ref, spec_ref, m3_ref, a1_ref, send_ref, a2_ref):
    for k in range(4):
        q = cols(k, DB)
        a2 = mm(m2_ref[...], recv_ref[:, q])
        a2_ref[:, q] = a2
        filt = (a2 * spec_ref[:, q].astype(F32)).astype(BF)
        send_ref[:, q] = mm(m3_ref[...], filt).astype(BF)
        if k == 1:
            send_ref.flush(0)
    send_ref.flush(1)
    send_ref[:, D:] = a1_ref[...]
    send_ref.flush()


def k_mid_back(recv_ref, m3t_ref, a2_ref, spec_ref, m2t_ref, da1_ref, sg_ref):
    for k in range(4):
        q = cols(k, DB)
        dfilt = mm(m3t_ref[...], recv_ref[:, q])
        sg_ref[:, q] = (dfilt * a2_ref[:, q]).astype(BF)
        da2 = (dfilt * spec_ref[:, q].astype(F32)).astype(BF)
        da1_ref[:, q] = mm(m2t_ref[...], da2).astype(BF)
        da1_ref.flush(k)


def cols(b, n):
    return slice(b * n, (b + 1) * n)


def hcols(b, k):
    return slice(k * HB + b * NJ, k * HB + (b + 1) * NJ)


def k_ahead(x_ref, gain_ref, mix_ref, g_ref, down_ref, m4_ref, n1_ref, gate_ref, dhid_ref, x_out, m4_out):
    x = x_ref[...].astype(F32)
    n1_ref[...] = (x * rms(x) * gain_ref[...]).astype(BF)
    for b in range(NB):
        gate_ref[:, cols(b, DB)] = mm(n1_ref[:, cols(b, DB)], mix_ref[cols(b, DB), :])
        dhs = mm_nt(g_ref[:, cols(b, DB)], down_ref[cols(b, HB), :]).astype(BF)
        for k in range(NB):
            dhid_ref[:, hcols(b, k)] = dhs[:, cols(k, NJ)]
    x_out[...] = x_ref[...]
    m4_out[...] = m4_ref[...]


def k_tail_back(
    recv_ref, m4_ref, x_ref, gate_ref, gain_ref, m2_ref, spec_ref, m3_ref, up_ref, act_ref,
    dhid_ref, g_ref, m4t_ref,
    send_ref, dy1_ref, dgate_ref, n2_ref, hs_ref, dup_ref, dact_ref,
    y1_ref, dn2_ref, b2_ref, up2_ref, act2_ref, db2_ref, r2_ref,
):
    b2_ref[...] = mm(m4_ref[...], recv_ref[:, :D])
    gain = gain_ref[...]
    for q in rows_of(16):
        y1 = (x_ref[q, :].astype(F32) + b2_ref[q, :] * gate_ref[q, :]).astype(BF).astype(F32)
        y1_ref[q, :] = y1
        r2 = rms(y1)
        r2_ref[q, :] = r2
        n2_ref[q, :] = (y1 * r2 * gain).astype(BF)
    n2_ref.flush()

    def lift(b):
        n2 = n2_ref[:, cols(b, DB)]
        up2_ref[b % 2] = mm(n2, up_ref[cols(b, DB), :])
        act2_ref[b % 2] = mm(n2, act_ref[cols(b, DB), :])

    def lower(b):
        dn2_ref[:, cols(b, DB)] = mm_nt(dup_ref[:, cols(b, HB)], up_ref[cols(b, DB), :]) + mm_nt(
            dact_ref[:, cols(b, HB)], act_ref[cols(b, DB), :]
        )

    def follow(k):
        a2 = mm(m2_ref[...], recv_ref[:, cols(4 + k, DB)])
        filt = (a2 * spec_ref[:, cols(k, DB)].astype(F32)).astype(BF)
        send_ref[:, cols(4 + k, DB)] = mm(m3_ref[...], filt).astype(BF)

    for w in (m2_ref, spec_ref, m3_ref, up_ref, act_ref, dhid_ref):
        w.get()
    lift(0)
    for b in range(NB):
        if b + 1 < NB:
            lift(b + 1)
        if b > 0:
            lower(b - 1)
        follow(b)
        for q in rows_of(32):
            up, act = up2_ref[b % 2, q, :], act2_ref[b % 2, q, :]
            sg = jax.nn.sigmoid(act)
            silu = act * sg
            hid = (silu * up).astype(BF)
            for k in range(NB):
                hs_ref[q, hcols(b, k)] = hid[:, cols(k, NJ)]
            dhid = dhid_ref[q, cols(b, HB)].astype(F32)
            dup_ref[q, cols(b, HB)] = (dhid * silu).astype(BF)
            dact_ref[q, cols(b, HB)] = (dhid * up * (sg + silu * (1.0 - sg))).astype(BF)
        dup_ref.flush(b)
        dact_ref.flush(b)
    lower(NB - 1)
    send_ref.flush(2)
    send_ref.flush(3)
    hs_ref.flush()
    for q in rows_of(16):
        s = gain * dn2_ref[q, :]
        y1, r2 = y1_ref[q, :], r2_ref[q, :]
        back = r2 * s - y1 * (r2 * r2 * r2) * jnp.mean(s * y1, axis=-1, keepdims=True)
        dy1 = (g_ref[q, :].astype(F32) + back).astype(BF)
        dy1_ref[q, :] = dy1
        dyw = dy1.astype(F32)
        db2_ref[q, :] = (dyw * gate_ref[q, :]).astype(BF)
        dgate_ref[q, :] = (dyw * b2_ref[q, :]).astype(BF)
    dy1_ref.flush()
    dgate_ref.flush()
    for k in range(4):
        send_ref[:, cols(k, DB)] = mm(m4t_ref[...], db2_ref[:, cols(k, DB)]).astype(BF)
        if k % 2:
            send_ref.flush(k // 2)


def k_grads(
    n1_ref, dgate_ref, mix_ref, n2_ref, dup_ref, dact_ref, hs_ref, g_ref,
    keep_ref, send_ref, dn1_ref, buf_ref, sems,
):
    core = lax.axis_index("seq") & 1

    def put(b, rows, value):
        w = value.astype(BF).reshape(4, 2, rows.stop - rows.start, DB)
        buf_ref[core, b, :, rows, :] = w[:, 0]
        buf_ref[1 - core, b, :, rows, :] = w[:, 1]

    copies = []
    for b in range(NB):
        dgate = dgate_ref[:, cols(b, DB)]
        put(b, slice(0, 32), mm(n1_ref[:, cols(b, DB)].T, dgate))
        dn1_ref[:, cols(b, DB)] = mm_nt(dgate, mix_ref[cols(b, DB), :])
        n2 = n2_ref[:, cols(b, DB)].T
        for k in range(2):
            put(b, slice(32 + 32 * k, 64 + 32 * k), mm(n2, dup_ref[:, cols(2 * b + k, DB)]))
            put(b, slice(96 + 32 * k, 128 + 32 * k), mm(n2, dact_ref[:, cols(2 * b + k, DB)]))
        put(b, slice(160, 224), mm(hs_ref[:, cols(b, HB)].T, g_ref[:, cols(b, DB)]))
        for side, out in enumerate((keep_ref, send_ref)):
            copy = pltpu.make_async_copy(buf_ref.at[side, b], out.at[b], sems.at[2 * b + side])
            copy.start()
            copies.append(copy)
    for copy in copies:
        copy.wait()


def ring_slots():
    i = lax.axis_index("seq")
    return i & 1, i >> 3, (i >> 1) & 3


def k_sum_core(keep_ref, recv_ref, *outs):
    core, x, y = ring_slots()
    keep = keep_ref.get()
    for d in range(4):
        for k in range(4):
            ix = jnp.where(core == 0, k, (x + d) & 3)
            iy = jnp.where(core == 0, (y + d) & 3, k)
            outs[d][k] = (keep[ix, iy].astype(F32) + recv_ref[ix, iy].astype(F32)).astype(BF)
        outs[d].flush()


def k_sum_ring(a_ref, b_ref, c_ref, d_ref, *outs):
    core, x, y = ring_slots()
    for d in range(4):
        k = (jnp.where(core == 0, x, y) + d) & 3
        outs[d][...] = (
            a_ref[k].astype(F32) + b_ref[k].astype(F32) + c_ref[k].astype(F32) + d_ref[k].astype(F32)
        ).astype(BF)


def k_sum_x(a_ref, b_ref, c_ref, d_ref, mix_ref, up_ref, act_ref, down_ref):
    def total(r):
        w = a_ref[r].astype(F32) + b_ref[r].astype(F32) + c_ref[r].astype(F32) + d_ref[r].astype(F32)
        return (w * KGRAD).astype(BF)

    mix_ref[...] = total(slice(0, 32))
    up_ref[:, :DB] = total(slice(32, 64))
    up_ref[:, DB:] = total(slice(64, 96))
    act_ref[:, :DB] = total(slice(96, 128))
    act_ref[:, DB:] = total(slice(128, 160))
    down_ref[...] = total(slice(160, 224))


def k_place(a_ref, b_ref, a_out, b_out, sems):
    copies = [
        pltpu.make_async_copy(a_ref, a_out.at[0], sems.at[0]),
        pltpu.make_async_copy(b_ref, b_out.at[0], sems.at[1]),
    ]
    for copy in copies:
        copy.start()
    for copy in copies:
        copy.wait()


def k_tail(recv_ref, m4_ref, x_ref, gain1_ref, mix_ref, gain2_ref, up_ref, act_ref, down_ref,
           out_ref, y1_ref, n_ref, hs_ref, gate_ref, b2_ref, up2_ref, act2_ref):
    gain1 = gain1_ref[...]
    for q in rows_of(16):
        x = x_ref[q, :].astype(F32)
        n_ref[q, :] = (x * rms(x) * gain1).astype(BF)
    for b in range(NB):
        b2_ref[:, cols(b, DB)] = mm(m4_ref[...], recv_ref[:, cols(4 + b, DB)])
        gate_ref[:, cols(b, DB)] = mm(n_ref[:, cols(b, DB)], mix_ref[cols(b, DB), :])
    gain2 = gain2_ref[...]
    for q in rows_of(16):
        y1 = (x_ref[q, :].astype(F32) + b2_ref[q, :] * gate_ref[q, :]).astype(BF).astype(F32)
        y1_ref[q, :] = y1
        n_ref[q, :] = (y1 * rms(y1) * gain2).astype(BF)

    def lift(b):
        n2 = n_ref[:, cols(b, DB)]
        up2_ref[b % 2] = mm(n2, up_ref[cols(b, DB), :])
        act2_ref[b % 2] = mm(n2, act_ref[cols(b, DB), :])

    lift(0)
    for b in range(NB):
        if b + 1 < NB:
            lift(b + 1)
        for q in rows_of(32):
            up, act = up2_ref[b % 2, q, :], act2_ref[b % 2, q, :]
            hid = (act * jax.nn.sigmoid(act) * up).astype(BF)
            for k in range(NB):
                hs_ref[q, hcols(b, k)] = hid[:, cols(k, NJ)]
    for b in range(NB):
        out_ref[:, cols(b, DB)] = (
            y1_ref[:, cols(b, DB)] + mm(hs_ref[:, cols(b, HB)], down_ref[cols(b, HB), :])
        ).astype(BF)


def k_end(recv_ref, m1t_ref, x_ref, gain_ref, dn1_ref, dy1_ref, dx_ref, w_ref):
    gain = gain_ref[...]
    for k in range(4):
        q = cols(k, DB)
        w_ref[:, q] = mm(m1t_ref[...], recv_ref[:, q]) + dn1_ref[:, q]
    for q in rows_of(16):
        x = x_ref[q, :].astype(F32)
        r1 = rms(x)
        s = gain * w_ref[q, :]
        back = r1 * s - x * (r1 * r1 * r1) * jnp.mean(s * x, axis=-1, keepdims=True)
        dx_ref[q, :] = (dy1_ref[q, :].astype(F32) + back).astype(BF)


def swap(v):
    return lax.all_to_all(v, "seq", split_axis=0, concat_axis=0, tiled=True)


def ring_y(i, d):
    return (i & 25) + ((((i >> 1) + d) & 3) << 1)


def ring_x(i, d):
    return (i + 8 * d) & 31


def ring(value, even, odd, d):
    pairs = [(i, odd(i, d) if i & 1 else even(i, d)) for i in range(32)]
    return lax.ppermute(value, "seq", pairs)


def shift(v, by):
    n = lax.axis_size("section")
    return lax.ppermute(v, "section", [(i, i + by) for i in range(n) if 0 <= i + by < n])


def shards(xa, xb, g, gain1, gain2, first, second, spec, third, fourth, mix, up, act, down):
    xa, xb, g = xa[0], xb[0], g[0]
    first, second, third, fourth = first[0], second[0], third[0], fourth[0]
    mix, up, act, down = mix[0], up[0], act[0], down[0]
    spec = spec[0].reshape(T, D)

    return body(xa, xb, g, gain1, gain2, first, second, spec, third, fourth, mix, up, act, down)


def h(*arrays):
    return [(a, "h") for a in arrays]


def v(*arrays):
    return [(a, "v") for a in arrays]


def front(x, gain, first):
    return call(
        k_front, [((T, D), BF, "c")], (first, "h"), (x, "x"), (gain, "h"),
        scratch=[pltpu.VMEM((T, D), BF)],
    )


def body(xa, xb, g, gain1, gain2, first, second, spec, third, fourth, mix, up, act, down):
    td, tt = (T, D), (T, T)
    (a1b,) = front(xb, gain1, first)
    r1 = swap(a1b)
    (a1a,) = front(xa, gain1, first)
    m1t, m2, m2t, m3, m3t, m4, m4t = call(
        k_prep, [(tt, BF, r) for r in "hvhvhhh"], *h(first, second, third, fourth)
    )
    send2, a2b = call(k_mid, [((T, 2 * D), BF, "c"), (td, F32, "h")], *v(r1, m2, spec, m3), *h(a1a))
    r2 = swap(send2)
    n1b, gateb, dhid, xb_v, m4_v = call(
        k_ahead,
        [(td, BF, "h"), (td, F32, "v"), ((T, FF), BF, "h"), (td, BF, "v"), (tt, BF, "v")],
        *h(xb, gain1, mix, g, down, m4),
    )
    send3, dy1, dgate, n2, hs, dup, dact = call(
        k_tail_back,
        [((T, 2 * D), BF, "c")]
        + [(td, BF, "h")] * 3
        + [((T, FF), BF, "h")]
        + [((T, FF), BF, "c")] * 2,
        *v(r2, m4_v, xb_v, gateb),
        *h(gain2, m2, spec, m3, up, act, dhid, g, m4t),
        scratch=[pltpu.VMEM(td, F32)] * 3
        + [pltpu.VMEM((2, T, HB), F32)] * 2
        + [pltpu.VMEM(td, BF), pltpu.VMEM((T, 1), F32)],
    )
    r3 = swap(send3)
    keep, other, dn1 = call(
        k_grads,
        [((4, 4, GR, DB), BF, "r"), ((4, 4, GR, DB), BF, "r"), (td, F32, "h")],
        *h(n1b, dgate, mix, n2, dup, dact, hs, g),
        scratch=[pltpu.VMEM((2, 4, 4, GR, DB), BF), pltpu.SemaphoreType.DMA((8,))],
    )
    other = lax.ppermute(other, "seq", [(i, i ^ 1) for i in range(32)])
    s0, *sy = call(k_sum_core, [((4, GR, DB), BF, "h")] * 4, *h(keep), *v(other))
    for d in (1, 3, 2):
        sy[d - 1] = ring(sy[d - 1], ring_y, ring_x, d)
    da1, sgrad = call(
        k_mid_back, [(td, BF, "c"), (td, BF, "h")], *v(r3), *h(m3t, a2b), *v(spec), *h(m2t)
    )
    r4 = swap(da1)
    (outa,) = call(
        k_tail, [(td, BF, "v")], *h(r3, m4, xa, gain1, mix, gain2, up, act, down),
        scratch=[pltpu.VMEM(td, F32), pltpu.VMEM(td, BF), pltpu.VMEM((T, FF), BF)]
        + [pltpu.VMEM(td, F32)] * 2
        + [pltpu.VMEM((2, T, HB), F32)] * 2,
    )
    next_input = shift(outa, 1)
    (dx,) = call(
        k_end, [(td, BF, "v")], *v(r4), *h(m1t, xb, gain1, dn1, dy1),
        scratch=[pltpu.VMEM(td, F32)],
    )
    upstream = shift(dx, -1)
    s0, *sx = call(k_sum_ring, [((GR, DB), BF, "v")] * 4, *h(s0), *v(*sy))
    sx = [ring(p, ring_x, ring_y, d + 1) for d, p in enumerate(sx)]
    gm, gu, ga, gd = call(
        k_sum_x,
        [((32, DB), BF, "h"), ((32, HB), BF, "h"), ((32, HB), BF, "h"), ((64, DB), BF, "h")],
        *v(s0, *sx),
    )
    next_input, upstream = call(
        k_place, [((1, T, D), BF, "r")] * 2, *v(next_input, upstream),
        scratch=[pltpu.SemaphoreType.DMA((2,))],
    )
    return (
        next_input,
        upstream,
        sgrad.reshape(1, NI, 4, D),
        gm[None],
        gu[None],
        ga[None],
        gd[None],
    )


def solution(mesh):
    in_specs = (
        P("section", "seq", None),
        P("section", "seq", None),
        P("section", "seq", None),
        P("section", None),
        P("section", None),
        P("section", "seq", None, None),
        P("section", "seq", None, None),
        P("section", None, "seq", None),
        P("section", "seq", None, None),
        P("section", "seq", None, None),
        P("section", None, None),
        P("section", None, None),
        P("section", None, None),
        P("section", None, None),
    )
    out_specs = (
        P("section", "seq", None),
        P("section", "seq", None),
        P("section", None, "seq", None),
        P("section", "seq", None),
        P("section", "seq", None),
        P("section", "seq", None),
        P("section", "seq", None),
    )
    return jax.shard_map(shards, mesh=mesh, in_specs=in_specs, out_specs=out_specs, check_vma=False)
```

```python
import math

import jax
import jax.numpy as jnp
from jax import lax
from jax.experimental import pallas as pl
from jax.experimental.pallas import tpu as pltpu
from jax.sharding import PartitionSpec as P

NB = 4
NI = 64
NJ = 128
D = 1024
FF = 2048
T = 256
HB = FF // NB
DB = D // NB
EPS = 1e-06
KGRAD = 1.0 / math.sqrt(NI * NJ)
GR = 224

F32 = jnp.float32
BF = jnp.bfloat16


def mm(a, b):
    return lax.dot_general(a, b, (((1,), (0,)), ((), ())), preferred_element_type=F32)


def mm_nt(a, b):
    return lax.dot_general(a, b, (((1,), (1,)), ((), ())), preferred_element_type=F32)


def iota(shape, dim):
    return lax.broadcasted_iota(jnp.int32, shape, dim)


def onehot(cond):
    return jnp.where(cond, 1.0, 0.0).astype(BF)


def r_half(r):
    return (r >> 2) & 1


def r_col(r):
    return ((r >> 3) << 2) + (r & 3)


class Lazy:
    def __init__(self, copies, ref):
        self.copies, self.ref, self.waited = copies, ref, set()

    def get(self, part=None):
        for k in range(len(self.copies)) if part is None else (part,):
            if k not in self.waited:
                self.copies[k].wait()
                self.waited.add(k)
        return self.ref

    def __getitem__(self, index):
        return self.get()[index]


class Late:
    def __init__(self, copies, ref):
        self.copies, self.ref, self.started = copies, ref, set()

    def __getitem__(self, index):
        return self.ref[index]

    def __setitem__(self, index, value):
        self.ref[index] = value

    def flush(self, part=None):
        for k in range(len(self.copies)) if part is None else (part,):
            if k not in self.started:
                self.copies[k].start()
                self.started.add(k)


PARTS = {"h": None, "x": 0, "c": 1}


def cuts(src, dst, sems, at, role, shape):
    if role == "h":
        return [pltpu.make_async_copy(src, dst, sems.at[at])]
    n = shape[PARTS[role]] // 4
    parts = [(slice(None),) * PARTS[role] + (pl.ds(k * n, n),) for k in range(4)]
    return [
        pltpu.make_async_copy(src.at[p], dst.at[p], sems.at[at + k]) for k, p in enumerate(parts)
    ]


def call(kernel, outs, *args, scratch=(), mib=40):
    arrays = [a for a, _ in args]
    in_roles, out_roles = [r for _, r in args], [o[2] for o in outs]
    n_in, n_out = len(args), len(outs)
    ins_h = [i for i, r in enumerate(in_roles) if r in PARTS]
    outs_h = [i for i, r in enumerate(out_roles) if r in PARTS]
    vm, hb = pl.BlockSpec(memory_space=pltpu.VMEM), pl.BlockSpec(memory_space=pltpu.HBM)
    bufs = [pltpu.VMEM(arrays[i].shape, arrays[i].dtype) for i in ins_h]
    bufs += [pltpu.VMEM(outs[i][0], outs[i][1]) for i in outs_h]
    n_buf = len(bufs)

    def body(*refs):
        ins, results = list(refs[:n_in]), list(refs[n_in : n_in + n_out])
        vmem = refs[n_in + n_out : n_in + n_out + n_buf]
        sems = refs[n_in + n_out + n_buf]
        rest = refs[n_in + n_out + n_buf + 1 :]
        at = 0
        for k, i in enumerate(ins_h):
            ins[i] = Lazy(cuts(ins[i], vmem[k], sems, at, in_roles[i], arrays[i].shape), vmem[k])
            at += 4
        for part in range(4):
            for i in ins_h:
                for copy in ins[i].copies[part : part + 1]:
                    copy.start()
        for k, i in enumerate(outs_h, len(ins_h)):
            copies = cuts(vmem[k], results[i], sems, at, out_roles[i], outs[i][0])
            results[i] = Late(copies, vmem[k])
            at += 4
        kernel(*ins, *results, *rest)
        for i in ins_h:
            ins[i].get()
        for i in outs_h:
            results[i].flush()
        for i in outs_h:
            for copy in results[i].copies:
                copy.wait()

    return pl.pallas_call(
        body,
        out_shape=[
            (jax.ShapeDtypeStruct if o[2] == "v" else pltpu.HBM)(o[0], o[1]) for o in outs
        ],
        in_specs=[vm if r == "v" else hb for r in in_roles],
        out_specs=[vm if r == "v" else hb for r in out_roles],
        scratch_shapes=bufs + [pltpu.SemaphoreType.DMA((4 * max(n_buf, 1),))] + list(scratch),
        compiler_params=pltpu.CompilerParams(vmem_limit_bytes=mib << 20),
    )(*(a if r == "v" else pltpu.with_memory_space_constraint(a, pltpu.HBM) for a, r in args))


def rows_of(n):
    return [slice(r, r + n) for r in range(0, T, n)]


def rms(v):
    return lax.rsqrt(jnp.mean(v * v, axis=-1, keepdims=True) + EPS)


def first_rows(first):
    w = first.reshape(T, NJ)
    r, t = iota((T, T), 0), iota((T, T), 1)
    pick = onehot(t == (r_half(r) << 7) + r_col(r))
    return mm(pick, w).astype(BF)


def k_front(first_ref, x_ref, gain_ref, a1_ref, n1_ref):
    rows = first_rows(first_ref[...])
    r, c = iota((T, T), 0), iota((T, T), 1)
    m1 = jnp.where((c >> 7) == r_half(r), jnp.concatenate([rows, rows], axis=1), 0).astype(BF)
    gain = gain_ref[...]
    for k in range(4):
        x_ref.get(k)
        for q in rows_of(16)[4 * k : 4 * k + 4]:
            x = x_ref.ref[q, :].astype(F32)
            n1_ref[q, :] = (x * rms(x) * gain).astype(BF)
    for k in range(4):
        a1_ref[:, cols(k, DB)] = mm(m1, n1_ref[:, cols(k, DB)]).astype(BF)
        a1_ref.flush(k)


def k_prep(first_ref, second_ref, third_ref, fourth_ref, m1t, m2, m2t, m3, m3t, m4, m4t):
    r, c = iota((T, T), 0), iota((T, T), 1)

    rows = first_rows(first_ref[...])
    e1t = onehot((iota((T, NJ), 0) & 127) == iota((T, NJ), 1))
    m1t[...] = jnp.where((r >> 7) == r_half(c), mm_nt(e1t, rows), 0.0).astype(BF)

    q = onehot(c == ((r & 3) << 6) + (r >> 2))
    e2 = onehot(iota((NI, T), 0) == (iota((NI, T), 1) >> 2))
    e2t = onehot((iota((T, NI), 0) >> 2) == iota((T, NI), 1))
    same = (r & 3) == (c & 3)
    for src, out, out_t in ((second_ref, m2, m2t), (third_ref, m3, m3t)):
        w = mm(q, src[...].reshape(T, NI)).astype(BF)
        out[...] = jnp.where(same, mm(w, e2), 0.0).astype(BF)
        out_t[...] = jnp.where(same, mm_nt(e2t, w), 0.0).astype(BF)

    w4 = fourth_ref[...].reshape(T, NJ)
    e4 = onehot(iota((NJ, T), 0) == r_col(iota((NJ, T), 1)))
    e4t = onehot(r_col(iota((T, NJ), 0)) == iota((T, NJ), 1))
    m4[...] = jnp.where((r >> 7) == r_half(c), mm(w4, e4), 0.0).astype(BF)
    m4t[...] = jnp.where(r_half(r) == (c >> 7), mm_nt(e4t, w4), 0.0).astype(BF)


def k_mid(recv_ref, m2_ref, spec_ref, m3_ref, a1_ref, send_ref, a2_ref):
    for k in range(4):
        q = cols(k, DB)
        a2 = mm(m2_ref[...], recv_ref[:, q])
        a2_ref[:, q] = a2
        filt = (a2 * spec_ref[:, q].astype(F32)).astype(BF)
        send_ref[:, q] = mm(m3_ref[...], filt).astype(BF)
        if k == 1:
            send_ref.flush(0)
    send_ref.flush(1)
    send_ref[:, D:] = a1_ref[...]
    send_ref.flush()


def k_mid_back(recv_ref, m3t_ref, a2_ref, spec_ref, m2t_ref, da1_ref, sg_ref, df_ref):
    for k in range(4):
        q = cols(k, DB)
        df_ref[:, q] = mm(m3t_ref[...], recv_ref[:, q])
        da2 = (df_ref[:, q] * spec_ref[:, q].astype(F32)).astype(BF)
        da1_ref[:, q] = mm(m2t_ref[...], da2).astype(BF)
        da1_ref.flush(k)
    for k in range(4):
        q = cols(k, DB)
        a2_ref.get(k)
        sg_ref[:, q] = (df_ref[:, q] * a2_ref.ref[:, q]).astype(BF)
        sg_ref.flush(k)


def cols(b, n):
    return slice(b * n, (b + 1) * n)


def hcols(b, k):
    return slice(k * HB + b * NJ, k * HB + (b + 1) * NJ)


def k_ahead(x_ref, gain_ref, mix_ref, g_ref, down_ref, m4_ref, n1_ref, gate_ref, dhid_ref, x_out, m4_out):
    x = x_ref[...].astype(F32)
    n1_ref[...] = (x * rms(x) * gain_ref[...]).astype(BF)
    for b in range(NB):
        gate_ref[:, cols(b, DB)] = mm(n1_ref[:, cols(b, DB)], mix_ref[cols(b, DB), :])
        dhs = mm_nt(g_ref[:, cols(b, DB)], down_ref[cols(b, HB), :]).astype(BF)
        for k in range(NB):
            dhid_ref[:, hcols(b, k)] = dhs[:, cols(k, NJ)]
    x_out[...] = x_ref[...]
    m4_out[...] = m4_ref[...]


def k_tail_back(
    recv_ref, m4_ref, x_ref, gate_ref, gain_ref, m2_ref, spec_ref, m3_ref, up_ref, act_ref,
    dhid_ref, g_ref, m4t_ref,
    send_ref, dy1_ref, dgate_ref, n2_ref, hs_ref, dup_ref, dact_ref,
    y1_ref, dn2_ref, b2_ref, up2_ref, act2_ref, db2_ref, r2_ref,
):
    b2_ref[...] = mm(m4_ref[...], recv_ref[:, :D])
    gain = gain_ref[...]
    for q in rows_of(16):
        y1 = (x_ref[q, :].astype(F32) + b2_ref[q, :] * gate_ref[q, :]).astype(BF).astype(F32)
        y1_ref[q, :] = y1
        r2 = rms(y1)
        r2_ref[q, :] = r2
        n2_ref[q, :] = (y1 * r2 * gain).astype(BF)
    n2_ref.flush()

    def lift(b):
        n2 = n2_ref[:, cols(b, DB)]
        up2_ref[b % 2] = mm(n2, up_ref[cols(b, DB), :])
        act2_ref[b % 2] = mm(n2, act_ref[cols(b, DB), :])

    def lower(b):
        dn2_ref[:, cols(b, DB)] = mm_nt(dup_ref[:, cols(b, HB)], up_ref[cols(b, DB), :]) + mm_nt(
            dact_ref[:, cols(b, HB)], act_ref[cols(b, DB), :]
        )

    def follow(k):
        a2 = mm(m2_ref[...], recv_ref[:, cols(4 + k, DB)])
        filt = (a2 * spec_ref[:, cols(k, DB)].astype(F32)).astype(BF)
        send_ref[:, cols(4 + k, DB)] = mm(m3_ref[...], filt).astype(BF)

    for w in (m2_ref, spec_ref, m3_ref, up_ref, act_ref, dhid_ref):
        w.get()
    lift(0)
    for b in range(NB):
        if b + 1 < NB:
            lift(b + 1)
        if b > 0:
            lower(b - 1)
        follow(b)
        for q in rows_of(32):
            up, act = up2_ref[b % 2, q, :], act2_ref[b % 2, q, :]
            sg = jax.nn.sigmoid(act)
            silu = act * sg
            hid = (silu * up).astype(BF)
            for k in range(NB):
                hs_ref[q, hcols(b, k)] = hid[:, cols(k, NJ)]
            dhid = dhid_ref[q, cols(b, HB)].astype(F32)
            dup_ref[q, cols(b, HB)] = (dhid * silu).astype(BF)
            dact_ref[q, cols(b, HB)] = (dhid * up * (sg + silu * (1.0 - sg))).astype(BF)
        dup_ref.flush(b)
        dact_ref.flush(b)
    lower(NB - 1)
    send_ref.flush(2)
    send_ref.flush(3)
    hs_ref.flush()
    for q in rows_of(16):
        s = gain * dn2_ref[q, :]
        y1, r2 = y1_ref[q, :], r2_ref[q, :]
        back = r2 * s - y1 * (r2 * r2 * r2) * jnp.mean(s * y1, axis=-1, keepdims=True)
        dy1 = (g_ref[q, :].astype(F32) + back).astype(BF)
        dy1_ref[q, :] = dy1
        dyw = dy1.astype(F32)
        db2_ref[q, :] = (dyw * gate_ref[q, :]).astype(BF)
        dgate_ref[q, :] = (dyw * b2_ref[q, :]).astype(BF)
    dy1_ref.flush()
    dgate_ref.flush()
    for k in range(4):
        send_ref[:, cols(k, DB)] = mm(m4t_ref[...], db2_ref[:, cols(k, DB)]).astype(BF)
        if k % 2:
            send_ref.flush(k // 2)


def k_grads(
    n1_ref, dgate_ref, mix_ref, n2_ref, dup_ref, dact_ref, hs_ref, g_ref,
    keep_ref, send_ref, dn1_ref, buf_ref, sems,
):
    core = lax.axis_index("seq") & 1

    def put(b, rows, value):
        w = value.astype(BF).reshape(4, 2, rows.stop - rows.start, DB)
        buf_ref[core, b, :, rows, :] = w[:, 0]
        buf_ref[1 - core, b, :, rows, :] = w[:, 1]

    copies = []
    for b in range(NB):
        for w in (n1_ref, dgate_ref, mix_ref, n2_ref, dup_ref, dact_ref, hs_ref, g_ref):
            w.get(b)
        dgate = dgate_ref.ref[:, cols(b, DB)]
        put(b, slice(0, 32), mm(n1_ref.ref[:, cols(b, DB)].T, dgate))
        dn1_ref[:, cols(b, DB)] = mm_nt(dgate, mix_ref.ref[cols(b, DB), :])
        dn1_ref.flush(b)
        n2 = n2_ref.ref[:, cols(b, DB)].T
        for k in range(2):
            put(b, slice(32 + 32 * k, 64 + 32 * k), mm(n2, dup_ref.ref[:, cols(2 * b + k, DB)]))
            put(b, slice(96 + 32 * k, 128 + 32 * k), mm(n2, dact_ref.ref[:, cols(2 * b + k, DB)]))
        put(b, slice(160, 224), mm(hs_ref.ref[:, cols(b, HB)].T, g_ref.ref[:, cols(b, DB)]))
        for side, out in enumerate((keep_ref, send_ref)):
            copy = pltpu.make_async_copy(buf_ref.at[side, b], out.at[b], sems.at[2 * b + side])
            copy.start()
            copies.append(copy)
    for copy in copies:
        copy.wait()


def ring_slots():
    i = lax.axis_index("seq")
    return i & 1, i >> 3, (i >> 1) & 3


def k_sum_core(keep_ref, recv_ref, m3t_ref, m2t_ref, *outs):
    core, x, y = ring_slots()
    keep = keep_ref.get()
    for d in range(4):
        for k in range(4):
            ix = jnp.where(core == 0, k, (x + d) & 3)
            iy = jnp.where(core == 0, (y + d) & 3, k)
            outs[d][k] = (keep[ix, iy].astype(F32) + recv_ref[ix, iy].astype(F32)).astype(BF)
        outs[d].flush()
    outs[4][...] = m3t_ref[...]
    outs[5][...] = m2t_ref[...]


def k_sum_ring(a_ref, b_ref, c_ref, d_ref, *outs):
    core, x, y = ring_slots()
    for d in range(4):
        k = (jnp.where(core == 0, x, y) + d) & 3
        outs[d][...] = (
            a_ref[k].astype(F32) + b_ref[k].astype(F32) + c_ref[k].astype(F32) + d_ref[k].astype(F32)
        ).astype(BF)
    outs[0].flush()


def k_sum_x(a_ref, b_ref, c_ref, d_ref, mix_ref, up_ref, act_ref, down_ref):
    def total(r):
        w = a_ref[r].astype(F32) + b_ref[r].astype(F32) + c_ref[r].astype(F32) + d_ref[r].astype(F32)
        return (w * KGRAD).astype(BF)

    mix_ref[...] = total(slice(0, 32))
    up_ref[:, :DB] = total(slice(32, 64))
    up_ref[:, DB:] = total(slice(64, 96))
    act_ref[:, :DB] = total(slice(96, 128))
    act_ref[:, DB:] = total(slice(128, 160))
    down_ref[...] = total(slice(160, 224))


def k_place(a_ref, b_ref, a_out, b_out, zero_ref, sems):
    section = lax.axis_index("section")
    ends = ((a_ref, a_out, 0), (b_ref, b_out, lax.axis_size("section") - 1))
    for k, (src, out, end) in enumerate(ends):

        @pl.when(section != end)
        def _():
            pltpu.make_async_copy(src, out.at[0], sems.at[k]).start()

        @pl.when(section == end)
        def _():
            zero_ref[...] = jnp.zeros_like(zero_ref)
            pltpu.make_async_copy(zero_ref, out.at[0], sems.at[k]).start()

    for k, (src, out, end) in enumerate(ends):
        pltpu.make_async_copy(src, out.at[0], sems.at[k]).wait()


def k_tail(recv_ref, m4_ref, x_ref, gain1_ref, mix_ref, gain2_ref, up_ref, act_ref, down_ref,
           out_ref, y1_ref, n_ref, hs_ref, gate_ref, b2_ref, up2_ref, act2_ref):
    gain1 = gain1_ref[...]
    for q in rows_of(16):
        x = x_ref[q, :].astype(F32)
        n_ref[q, :] = (x * rms(x) * gain1).astype(BF)
    for b in range(NB):
        b2_ref[:, cols(b, DB)] = mm(m4_ref[...], recv_ref[:, cols(4 + b, DB)])
        gate_ref[:, cols(b, DB)] = mm(n_ref[:, cols(b, DB)], mix_ref[cols(b, DB), :])
    gain2 = gain2_ref[...]
    for q in rows_of(16):
        y1 = (x_ref[q, :].astype(F32) + b2_ref[q, :] * gate_ref[q, :]).astype(BF).astype(F32)
        y1_ref[q, :] = y1
        n_ref[q, :] = (y1 * rms(y1) * gain2).astype(BF)

    def lift(b):
        n2 = n_ref[:, cols(b, DB)]
        up2_ref[b % 2] = mm(n2, up_ref[cols(b, DB), :])
        act2_ref[b % 2] = mm(n2, act_ref[cols(b, DB), :])

    lift(0)
    for b in range(NB):
        if b + 1 < NB:
            lift(b + 1)
        for q in rows_of(32):
            up, act = up2_ref[b % 2, q, :], act2_ref[b % 2, q, :]
            hid = (act * jax.nn.sigmoid(act) * up).astype(BF)
            for k in range(NB):
                hs_ref[q, hcols(b, k)] = hid[:, cols(k, NJ)]
    for b in range(NB):
        out_ref[:, cols(b, DB)] = (
            y1_ref[:, cols(b, DB)] + mm(hs_ref[:, cols(b, HB)], down_ref[cols(b, HB), :])
        ).astype(BF)


def k_end(recv_ref, m1t_ref, x_ref, gain_ref, dn1_ref, dy1_ref, dx_ref, w_ref):
    gain = gain_ref[...]
    for k in range(4):
        q = cols(k, DB)
        w_ref[:, q] = mm(m1t_ref[...], recv_ref[:, q]) + dn1_ref[:, q]
    for q in rows_of(16):
        x = x_ref[q, :].astype(F32)
        r1 = rms(x)
        s = gain * w_ref[q, :]
        back = r1 * s - x * (r1 * r1 * r1) * jnp.mean(s * x, axis=-1, keepdims=True)
        dx_ref[q, :] = (dy1_ref[q, :].astype(F32) + back).astype(BF)


def swap(v):
    return lax.all_to_all(v, "seq", split_axis=0, concat_axis=0, tiled=True)


def ring_y(i, d):
    return (i & 25) + ((((i >> 1) + d) & 3) << 1)


def ring_x(i, d):
    return (i + 8 * d) & 31


def ring(value, even, odd, d):
    pairs = [(i, odd(i, d) if i & 1 else even(i, d)) for i in range(32)]
    return lax.ppermute(value, "seq", pairs)


def shift(v, by):
    n = lax.axis_size("section")
    pairs = [(i, (i + by) % n) for i in range(n) if by > 0 or i + by >= 0]
    return lax.ppermute(v, "section", pairs)


def shards(xa, xb, g, gain1, gain2, first, second, spec, third, fourth, mix, up, act, down):
    xa, xb, g = xa[0], xb[0], g[0]
    first, second, third, fourth = first[0], second[0], third[0], fourth[0]
    mix, up, act, down = mix[0], up[0], act[0], down[0]
    spec = spec[0].reshape(T, D)

    return body(xa, xb, g, gain1, gain2, first, second, spec, third, fourth, mix, up, act, down)


def h(*arrays):
    return [(a, "h") for a in arrays]


def v(*arrays):
    return [(a, "v") for a in arrays]


def front(x, gain, first):
    return call(
        k_front, [((T, D), BF, "c")], (first, "h"), (x, "x"), (gain, "h"),
        scratch=[pltpu.VMEM((T, D), BF)],
    )


def body(xa, xb, g, gain1, gain2, first, second, spec, third, fourth, mix, up, act, down):
    td, tt = (T, D), (T, T)
    (a1b,) = front(xb, gain1, first)
    r1 = swap(a1b)
    (a1a,) = front(xa, gain1, first)
    m1t, m2, m2t, m3, m3t, m4, m4t = call(
        k_prep, [(tt, BF, r) for r in "hvhvhhh"], *h(first, second, third, fourth)
    )
    send2, a2b = call(k_mid, [((T, 2 * D), BF, "c"), (td, F32, "h")], *v(r1, m2, spec, m3), *h(a1a))
    r2 = swap(send2)
    n1b, gateb, dhid, xb_v, m4_v = call(
        k_ahead,
        [(td, BF, "h"), (td, F32, "v"), ((T, FF), BF, "h"), (td, BF, "v"), (tt, BF, "v")],
        *h(xb, gain1, mix, g, down, m4),
    )
    send3, dy1, dgate, n2, hs, dup, dact = call(
        k_tail_back,
        [((T, 2 * D), BF, "c")]
        + [(td, BF, "h")] * 3
        + [((T, FF), BF, "h")]
        + [((T, FF), BF, "c")] * 2,
        *v(r2, m4_v, xb_v, gateb),
        *h(gain2, m2, spec, m3, up, act, dhid, g, m4t),
        scratch=[pltpu.VMEM(td, F32)] * 3
        + [pltpu.VMEM((2, T, HB), F32)] * 2
        + [pltpu.VMEM(td, BF), pltpu.VMEM((T, 1), F32)],
    )
    r3 = swap(send3)
    keep, other, dn1 = call(
        k_grads,
        [((4, 4, GR, DB), BF, "r"), ((4, 4, GR, DB), BF, "r"), (td, F32, "c")],
        *((w, "x" if w is mix else "c") for w in (n1b, dgate, mix, n2, dup, dact, hs, g)),
        scratch=[pltpu.VMEM((2, 4, 4, GR, DB), BF), pltpu.SemaphoreType.DMA((8,))],
    )
    other = lax.ppermute(other, "seq", [(i, i ^ 1) for i in range(32)])
    s0, *sy, m3t, m2t = call(
        k_sum_core, [((4, GR, DB), BF, "h")] * 4 + [(tt, BF, "v")] * 2,
        *h(keep), *v(other), *h(m3t, m2t),
    )
    for d in (1, 3, 2):
        sy[d - 1] = ring(sy[d - 1], ring_y, ring_x, d)
    da1, sgrad = call(
        k_mid_back, [(td, BF, "c")] * 2, *v(r3, m3t), (a2b, "c"), *v(spec, m2t),
        scratch=[pltpu.VMEM(td, F32)],
    )
    r4 = swap(da1)
    (outa,) = call(
        k_tail, [(td, BF, "v")], *h(r3, m4, xa, gain1, mix, gain2, up, act, down),
        scratch=[pltpu.VMEM(td, F32), pltpu.VMEM(td, BF), pltpu.VMEM((T, FF), BF)]
        + [pltpu.VMEM(td, F32)] * 2
        + [pltpu.VMEM((2, T, HB), F32)] * 2,
    )
    next_input = shift(outa, 1)
    (dx,) = call(
        k_end, [(td, BF, "v")], *v(r4), *h(m1t, xb, gain1, dn1, dy1),
        scratch=[pltpu.VMEM(td, F32)],
    )
    upstream = shift(dx, -1)
    s0, *sx = call(k_sum_ring, [((GR, DB), BF, r) for r in "hvvv"], *h(s0), *v(*sy))
    sx = [ring(p, ring_x, ring_y, d + 1) for d, p in enumerate(sx)]
    gm, gu, ga, gd = call(
        k_sum_x,
        [((32, DB), BF, "h"), ((32, HB), BF, "h"), ((32, HB), BF, "h"), ((64, DB), BF, "h")],
        *h(s0), *v(*sx),
    )
    next_input, upstream = call(
        k_place, [((1, T, D), BF, "r")] * 2, *v(next_input, upstream),
        scratch=[pltpu.VMEM(td, BF), pltpu.SemaphoreType.DMA((2,))],
    )
    return (
        next_input,
        upstream,
        sgrad.reshape(1, NI, 4, D),
        gm[None],
        gu[None],
        ga[None],
        gd[None],
    )


def solution(mesh):
    in_specs = (
        P("section", "seq", None),
        P("section", "seq", None),
        P("section", "seq", None),
        P("section", None),
        P("section", None),
        P("section", "seq", None, None),
        P("section", "seq", None, None),
        P("section", None, "seq", None),
        P("section", "seq", None, None),
        P("section", "seq", None, None),
        P("section", None, None),
        P("section", None, None),
        P("section", None, None),
        P("section", None, None),
    )
    out_specs = (
        P("section", "seq", None),
        P("section", "seq", None),
        P("section", None, "seq", None),
        P("section", "seq", None),
        P("section", "seq", None),
        P("section", "seq", None),
        P("section", "seq", None),
    )
    return jax.shard_map(shards, mesh=mesh, in_specs=in_specs, out_specs=out_specs, check_vma=False)
```

```python
import math

import jax
import jax.numpy as jnp
from jax import lax
from jax.experimental import pallas as pl
from jax.experimental.pallas import tpu as pltpu
from jax.sharding import PartitionSpec as P

NB = 4
NI = 64
NJ = 128
D = 1024
FF = 2048
T = 256
HB = FF // NB
DB = D // NB
EPS = 1e-06
KGRAD = 1.0 / math.sqrt(NI * NJ)
GR = 224

F32 = jnp.float32
BF = jnp.bfloat16


def mm(a, b):
    return lax.dot_general(a, b, (((1,), (0,)), ((), ())), preferred_element_type=F32)


def mm_nt(a, b):
    return lax.dot_general(a, b, (((1,), (1,)), ((), ())), preferred_element_type=F32)


def iota(shape, dim):
    return lax.broadcasted_iota(jnp.int32, shape, dim)


def onehot(cond):
    return jnp.where(cond, 1.0, 0.0).astype(BF)


def r_half(r):
    return (r >> 2) & 1


def r_col(r):
    return ((r >> 3) << 2) + (r & 3)


class Lazy:
    def __init__(self, copies, ref):
        self.copies, self.ref, self.waited = copies, ref, set()

    def get(self, part=None):
        for k in range(len(self.copies)) if part is None else (part,):
            if k not in self.waited:
                self.copies[k].wait()
                self.waited.add(k)
        return self.ref

    def __getitem__(self, index):
        return self.get()[index]


class Late:
    def __init__(self, copies, ref):
        self.copies, self.ref, self.started = copies, ref, set()

    def __getitem__(self, index):
        return self.ref[index]

    def __setitem__(self, index, value):
        self.ref[index] = value

    def flush(self, part=None):
        for k in range(len(self.copies)) if part is None else (part,):
            if k not in self.started:
                self.copies[k].start()
                self.started.add(k)


PARTS = {"h": None, "x": 0, "c": 1}


def cuts(src, dst, sems, at, role, shape):
    if role == "h":
        return [pltpu.make_async_copy(src, dst, sems.at[at])]
    n = shape[PARTS[role]] // 4
    parts = [(slice(None),) * PARTS[role] + (pl.ds(k * n, n),) for k in range(4)]
    return [
        pltpu.make_async_copy(src.at[p], dst.at[p], sems.at[at + k]) for k, p in enumerate(parts)
    ]


def call(kernel, outs, *args, scratch=(), mib=40):
    arrays = [a for a, _ in args]
    in_roles, out_roles = [r for _, r in args], [o[2] for o in outs]
    n_in, n_out = len(args), len(outs)
    ins_h = [i for i, r in enumerate(in_roles) if r in PARTS]
    outs_h = [i for i, r in enumerate(out_roles) if r in PARTS]
    vm, hb = pl.BlockSpec(memory_space=pltpu.VMEM), pl.BlockSpec(memory_space=pltpu.HBM)
    bufs = [pltpu.VMEM(arrays[i].shape, arrays[i].dtype) for i in ins_h]
    bufs += [pltpu.VMEM(outs[i][0], outs[i][1]) for i in outs_h]
    n_buf = len(bufs)

    def body(*refs):
        ins, results = list(refs[:n_in]), list(refs[n_in : n_in + n_out])
        vmem = refs[n_in + n_out : n_in + n_out + n_buf]
        sems = refs[n_in + n_out + n_buf]
        rest = refs[n_in + n_out + n_buf + 1 :]
        at = 0
        for k, i in enumerate(ins_h):
            ins[i] = Lazy(cuts(ins[i], vmem[k], sems, at, in_roles[i], arrays[i].shape), vmem[k])
            at += 4
        for part in range(4):
            for i in ins_h:
                for copy in ins[i].copies[part : part + 1]:
                    copy.start()
        for k, i in enumerate(outs_h, len(ins_h)):
            copies = cuts(vmem[k], results[i], sems, at, out_roles[i], outs[i][0])
            results[i] = Late(copies, vmem[k])
            at += 4
        kernel(*ins, *results, *rest)
        for i in ins_h:
            ins[i].get()
        for i in outs_h:
            results[i].flush()
        for i in outs_h:
            for copy in results[i].copies:
                copy.wait()

    return pl.pallas_call(
        body,
        out_shape=[
            (jax.ShapeDtypeStruct if o[2] == "v" else pltpu.HBM)(o[0], o[1]) for o in outs
        ],
        in_specs=[vm if r == "v" else hb for r in in_roles],
        out_specs=[vm if r == "v" else hb for r in out_roles],
        scratch_shapes=bufs + [pltpu.SemaphoreType.DMA((4 * max(n_buf, 1),))] + list(scratch),
        compiler_params=pltpu.CompilerParams(vmem_limit_bytes=mib << 20),
    )(*(a if r == "v" else pltpu.with_memory_space_constraint(a, pltpu.HBM) for a, r in args))


def rows_of(n):
    return [slice(r, r + n) for r in range(0, T, n)]


def rms(v):
    return lax.rsqrt(jnp.mean(v * v, axis=-1, keepdims=True) + EPS)


def first_rows(first):
    w = first.reshape(T, NJ)
    r, t = iota((T, T), 0), iota((T, T), 1)
    pick = onehot(t == (r_half(r) << 7) + r_col(r))
    return mm(pick, w).astype(BF)


def k_front(first_ref, x_ref, gain_ref, a1_ref, n1_ref):
    rows = first_rows(first_ref[...])
    r, c = iota((T, T), 0), iota((T, T), 1)
    m1 = jnp.where((c >> 7) == r_half(r), jnp.concatenate([rows, rows], axis=1), 0).astype(BF)
    gain = gain_ref[...]
    for k in range(4):
        x_ref.get(k)
        for q in rows_of(16)[4 * k : 4 * k + 4]:
            x = x_ref.ref[q, :].astype(F32)
            n1_ref[q, :] = (x * rms(x) * gain).astype(BF)
    for k in range(4):
        a1_ref[:, cols(k, DB)] = mm(m1, n1_ref[:, cols(k, DB)]).astype(BF)
        a1_ref.flush(k)


def k_prep(first_ref, second_ref, third_ref, fourth_ref, m1t, m2, m2t, m3, m3t, m4, m4t):
    r, c = iota((T, T), 0), iota((T, T), 1)

    rows = first_rows(first_ref[...])
    e1t = onehot((iota((T, NJ), 0) & 127) == iota((T, NJ), 1))
    m1t[...] = jnp.where((r >> 7) == r_half(c), mm_nt(e1t, rows), 0.0).astype(BF)

    q = onehot(c == ((r & 3) << 6) + (r >> 2))
    e2 = onehot(iota((NI, T), 0) == (iota((NI, T), 1) >> 2))
    e2t = onehot((iota((T, NI), 0) >> 2) == iota((T, NI), 1))
    same = (r & 3) == (c & 3)
    for src, out, out_t in ((second_ref, m2, m2t), (third_ref, m3, m3t)):
        w = mm(q, src[...].reshape(T, NI)).astype(BF)
        out[...] = jnp.where(same, mm(w, e2), 0.0).astype(BF)
        out_t[...] = jnp.where(same, mm_nt(e2t, w), 0.0).astype(BF)

    w4 = fourth_ref[...].reshape(T, NJ)
    e4 = onehot(iota((NJ, T), 0) == r_col(iota((NJ, T), 1)))
    e4t = onehot(r_col(iota((T, NJ), 0)) == iota((T, NJ), 1))
    m4[...] = jnp.where((r >> 7) == r_half(c), mm(w4, e4), 0.0).astype(BF)
    m4t[...] = jnp.where(r_half(r) == (c >> 7), mm_nt(e4t, w4), 0.0).astype(BF)


def k_mid(recv_ref, m2_ref, spec_ref, m3_ref, a1_ref, send_ref, a2_ref):
    for k in range(4):
        q = cols(k, DB)
        a2 = mm(m2_ref[...], recv_ref[:, q])
        a2_ref[:, q] = a2
        filt = (a2 * spec_ref[:, q].astype(F32)).astype(BF)
        send_ref[:, q] = mm(m3_ref[...], filt).astype(BF)
        if k == 1:
            send_ref.flush(0)
    send_ref.flush(1)
    send_ref[:, D:] = a1_ref[...]
    send_ref.flush()


def k_mid_back(recv_ref, m3t_ref, a2_ref, spec_ref, m2t_ref, da1_ref, sg_ref, df_ref):
    for k in range(4):
        q = cols(k, DB)
        df_ref[:, q] = mm(m3t_ref[...], recv_ref[:, q])
        da2 = (df_ref[:, q] * spec_ref[:, q].astype(F32)).astype(BF)
        da1_ref[:, q] = mm(m2t_ref[...], da2).astype(BF)
        da1_ref.flush(k)
    for k in range(4):
        q = cols(k, DB)
        a2_ref.get(k)
        sg_ref[:, q] = (df_ref[:, q] * a2_ref.ref[:, q]).astype(BF)
        sg_ref.flush(k)


def cols(b, n):
    return slice(b * n, (b + 1) * n)


def hcols(b, k):
    return slice(k * HB + b * NJ, k * HB + (b + 1) * NJ)


def k_ahead(x_ref, gain_ref, mix_ref, g_ref, down_ref, m4_ref, n1_ref, gate_ref, dhid_ref, x_out, m4_out):
    x = x_ref[...].astype(F32)
    n1_ref[...] = (x * rms(x) * gain_ref[...]).astype(BF)
    for b in range(NB):
        gate_ref[:, cols(b, DB)] = mm(n1_ref[:, cols(b, DB)], mix_ref[cols(b, DB), :])
        dhs = mm_nt(g_ref[:, cols(b, DB)], down_ref[cols(b, HB), :]).astype(BF)
        for k in range(NB):
            dhid_ref[:, hcols(b, k)] = dhs[:, cols(k, NJ)]
    x_out[...] = x_ref[...]
    m4_out[...] = m4_ref[...]


def k_tail_back(
    recv_ref, m4_ref, x_ref, gate_ref, gain_ref, m2_ref, spec_ref, m3_ref, up_ref, act_ref,
    dhid_ref, g_ref, m4t_ref,
    send_ref, dy1_ref, dgate_ref, n2_ref, hs_ref, dup_ref, dact_ref,
    y1_ref, dn2_ref, b2_ref, up2_ref, act2_ref, db2_ref, r2_ref,
):
    b2_ref[...] = mm(m4_ref[...], recv_ref[:, :D])
    gain = gain_ref[...]
    for q in rows_of(16):
        y1 = (x_ref[q, :].astype(F32) + b2_ref[q, :] * gate_ref[q, :]).astype(BF).astype(F32)
        y1_ref[q, :] = y1
        r2 = rms(y1)
        r2_ref[q, :] = r2
        n2_ref[q, :] = (y1 * r2 * gain).astype(BF)
    n2_ref.flush()

    def lift(b):
        n2 = n2_ref[:, cols(b, DB)]
        up2_ref[b % 2] = mm(n2, up_ref[cols(b, DB), :])
        act2_ref[b % 2] = mm(n2, act_ref[cols(b, DB), :])

    def lower(b):
        dn2_ref[:, cols(b, DB)] = mm_nt(dup_ref[:, cols(b, HB)], up_ref[cols(b, DB), :]) + mm_nt(
            dact_ref[:, cols(b, HB)], act_ref[cols(b, DB), :]
        )

    def follow(k):
        a2 = mm(m2_ref[...], recv_ref[:, cols(4 + k, DB)])
        filt = (a2 * spec_ref[:, cols(k, DB)].astype(F32)).astype(BF)
        send_ref[:, cols(4 + k, DB)] = mm(m3_ref[...], filt).astype(BF)

    for w in (m2_ref, spec_ref, m3_ref):
        w.get()
    for b in range(NB):
        follow(b)
    send_ref.flush(2)
    send_ref.flush(3)
    for w in (up_ref, act_ref):
        w.get()
    lift(0)
    lift(1)
    dhid_ref.get()
    for b in range(NB):
        if 0 < b < NB - 1:
            lift(b + 1)
        if b > 0:
            lower(b - 1)
        for q in rows_of(32):
            up, act = up2_ref[b % 2, q, :], act2_ref[b % 2, q, :]
            sg = jax.nn.sigmoid(act)
            silu = act * sg
            hid = (silu * up).astype(BF)
            for k in range(NB):
                hs_ref[q, hcols(b, k)] = hid[:, cols(k, NJ)]
            dhid = dhid_ref[q, cols(b, HB)].astype(F32)
            dup_ref[q, cols(b, HB)] = (dhid * silu).astype(BF)
            dact_ref[q, cols(b, HB)] = (dhid * up * (sg + silu * (1.0 - sg))).astype(BF)
        dup_ref.flush(b)
        dact_ref.flush(b)
    lower(NB - 1)
    send_ref.flush(2)
    send_ref.flush(3)
    hs_ref.flush()
    for q in rows_of(16):
        s = gain * dn2_ref[q, :]
        y1, r2 = y1_ref[q, :], r2_ref[q, :]
        back = r2 * s - y1 * (r2 * r2 * r2) * jnp.mean(s * y1, axis=-1, keepdims=True)
        dy1 = (g_ref[q, :].astype(F32) + back).astype(BF)
        dy1_ref[q, :] = dy1
        dyw = dy1.astype(F32)
        db2_ref[q, :] = (dyw * gate_ref[q, :]).astype(BF)
        dgate_ref[q, :] = (dyw * b2_ref[q, :]).astype(BF)
    dy1_ref.flush()
    dgate_ref.flush()
    for k in range(4):
        send_ref[:, cols(k, DB)] = mm(m4t_ref[...], db2_ref[:, cols(k, DB)]).astype(BF)
        if k % 2:
            send_ref.flush(k // 2)


def k_grads(
    n1_ref, dgate_ref, mix_ref, n2_ref, dup_ref, dact_ref, hs_ref, g_ref,
    keep_ref, send_ref, dn1_ref, buf_ref, sems,
):
    core = lax.axis_index("seq") & 1

    def put(b, rows, value):
        w = value.astype(BF).reshape(4, 2, rows.stop - rows.start, DB)
        buf_ref[core, b, :, rows, :] = w[:, 0]
        buf_ref[1 - core, b, :, rows, :] = w[:, 1]

    copies = []
    for b in range(NB):
        for w in (n1_ref, dgate_ref, mix_ref, n2_ref, dup_ref, dact_ref, hs_ref, g_ref):
            w.get(b)
        dgate = dgate_ref.ref[:, cols(b, DB)]
        put(b, slice(0, 32), mm(n1_ref.ref[:, cols(b, DB)].T, dgate))
        dn1_ref[:, cols(b, DB)] = mm_nt(dgate, mix_ref.ref[cols(b, DB), :])
        dn1_ref.flush(b)
        n2 = n2_ref.ref[:, cols(b, DB)].T
        for k in range(2):
            put(b, slice(32 + 32 * k, 64 + 32 * k), mm(n2, dup_ref.ref[:, cols(2 * b + k, DB)]))
            put(b, slice(96 + 32 * k, 128 + 32 * k), mm(n2, dact_ref.ref[:, cols(2 * b + k, DB)]))
        put(b, slice(160, 224), mm(hs_ref.ref[:, cols(b, HB)].T, g_ref.ref[:, cols(b, DB)]))
        for side, out in enumerate((keep_ref, send_ref)):
            copy = pltpu.make_async_copy(buf_ref.at[side, b], out.at[b], sems.at[2 * b + side])
            copy.start()
            copies.append(copy)
    for copy in copies:
        copy.wait()


def ring_slots():
    i = lax.axis_index("seq")
    return i & 1, i >> 3, (i >> 1) & 3


def k_sum_core(keep_ref, recv_ref, m3t_ref, m2t_ref, *outs):
    core, x, y = ring_slots()
    keep = keep_ref.get()
    for d in range(4):
        for k in range(4):
            ix = jnp.where(core == 0, k, (x + d) & 3)
            iy = jnp.where(core == 0, (y + d) & 3, k)
            outs[d][k] = (keep[ix, iy].astype(F32) + recv_ref[ix, iy].astype(F32)).astype(BF)
        outs[d].flush()
    outs[4][...] = m3t_ref[...]
    outs[5][...] = m2t_ref[...]


def k_sum_ring(a_ref, b_ref, c_ref, d_ref, *outs):
    core, x, y = ring_slots()
    for d in range(4):
        k = (jnp.where(core == 0, x, y) + d) & 3
        outs[d][...] = (
            a_ref[k].astype(F32) + b_ref[k].astype(F32) + c_ref[k].astype(F32) + d_ref[k].astype(F32)
        ).astype(BF)
        if d == 0:
            outs[0].flush()


def k_sum_x(a_ref, b_ref, c_ref, d_ref, mix_ref, up_ref, act_ref, down_ref):
    def total(r):
        w = a_ref[r].astype(F32) + b_ref[r].astype(F32) + c_ref[r].astype(F32) + d_ref[r].astype(F32)
        return (w * KGRAD).astype(BF)

    mix_ref[...] = total(slice(0, 32))
    up_ref[:, :DB] = total(slice(32, 64))
    up_ref[:, DB:] = total(slice(64, 96))
    act_ref[:, :DB] = total(slice(96, 128))
    act_ref[:, DB:] = total(slice(128, 160))
    down_ref[...] = total(slice(160, 224))


def k_place(a_ref, b_ref, a_out, b_out, zero_ref, sems):
    section = lax.axis_index("section")
    ends = ((a_ref, a_out, 0), (b_ref, b_out, lax.axis_size("section") - 1))
    for k, (src, out, end) in enumerate(ends):

        @pl.when(section != end)
        def _():
            pltpu.make_async_copy(src, out.at[0], sems.at[k]).start()

        @pl.when(section == end)
        def _():
            zero_ref[...] = jnp.zeros_like(zero_ref)
            pltpu.make_async_copy(zero_ref, out.at[0], sems.at[k]).start()

    for k, (src, out, end) in enumerate(ends):
        pltpu.make_async_copy(src, out.at[0], sems.at[k]).wait()


def k_tail(recv_ref, m4_ref, x_ref, gain1_ref, mix_ref, gain2_ref, up_ref, act_ref, down_ref,
           out_ref, y1_ref, n_ref, hs_ref, gate_ref, b2_ref, up2_ref, act2_ref):
    gain1 = gain1_ref[...]
    for q in rows_of(16):
        x = x_ref[q, :].astype(F32)
        n_ref[q, :] = (x * rms(x) * gain1).astype(BF)
    for b in range(NB):
        b2_ref[:, cols(b, DB)] = mm(m4_ref[...], recv_ref[:, cols(4 + b, DB)])
        gate_ref[:, cols(b, DB)] = mm(n_ref[:, cols(b, DB)], mix_ref[cols(b, DB), :])
    gain2 = gain2_ref[...]
    for q in rows_of(16):
        y1 = (x_ref[q, :].astype(F32) + b2_ref[q, :] * gate_ref[q, :]).astype(BF).astype(F32)
        y1_ref[q, :] = y1
        n_ref[q, :] = (y1 * rms(y1) * gain2).astype(BF)

    def lift(b):
        n2 = n_ref[:, cols(b, DB)]
        up2_ref[b % 2] = mm(n2, up_ref[cols(b, DB), :])
        act2_ref[b % 2] = mm(n2, act_ref[cols(b, DB), :])

    lift(0)
    for b in range(NB):
        if b + 1 < NB:
            lift(b + 1)
        for q in rows_of(32):
            up, act = up2_ref[b % 2, q, :], act2_ref[b % 2, q, :]
            hid = (act * jax.nn.sigmoid(act) * up).astype(BF)
            for k in range(NB):
                hs_ref[q, hcols(b, k)] = hid[:, cols(k, NJ)]
    for b in range(NB):
        out_ref[:, cols(b, DB)] = (
            y1_ref[:, cols(b, DB)] + mm(hs_ref[:, cols(b, HB)], down_ref[cols(b, HB), :])
        ).astype(BF)


def k_end(recv_ref, m1t_ref, x_ref, gain_ref, dn1_ref, dy1_ref, dx_ref, w_ref):
    gain = gain_ref[...]
    for k in range(4):
        q = cols(k, DB)
        w_ref[:, q] = mm(m1t_ref[...], recv_ref[:, q]) + dn1_ref[:, q]
    for q in rows_of(16):
        x = x_ref[q, :].astype(F32)
        r1 = rms(x)
        s = gain * w_ref[q, :]
        back = r1 * s - x * (r1 * r1 * r1) * jnp.mean(s * x, axis=-1, keepdims=True)
        dx_ref[q, :] = (dy1_ref[q, :].astype(F32) + back).astype(BF)


def swap(v):
    return lax.all_to_all(v, "seq", split_axis=0, concat_axis=0, tiled=True)


def ring_y(i, d):
    return (i & 25) + ((((i >> 1) + d) & 3) << 1)


def ring_x(i, d):
    return (i + 8 * d) & 31


def ring(value, even, odd, d):
    pairs = [(i, odd(i, d) if i & 1 else even(i, d)) for i in range(32)]
    return lax.ppermute(value, "seq", pairs)


def shift(v, by):
    n = lax.axis_size("section")
    pairs = [(i, (i + by) % n) for i in range(n) if by > 0 or i + by >= 0]
    return lax.ppermute(v, "section", pairs)


def shards(xa, xb, g, gain1, gain2, first, second, spec, third, fourth, mix, up, act, down):
    xa, xb, g = xa[0], xb[0], g[0]
    first, second, third, fourth = first[0], second[0], third[0], fourth[0]
    mix, up, act, down = mix[0], up[0], act[0], down[0]
    spec = spec[0].reshape(T, D)

    return body(xa, xb, g, gain1, gain2, first, second, spec, third, fourth, mix, up, act, down)


def h(*arrays):
    return [(a, "h") for a in arrays]


def v(*arrays):
    return [(a, "v") for a in arrays]


def front(x, gain, first):
    return call(
        k_front, [((T, D), BF, "c")], (first, "h"), (x, "x"), (gain, "h"),
        scratch=[pltpu.VMEM((T, D), BF)],
    )


def body(xa, xb, g, gain1, gain2, first, second, spec, third, fourth, mix, up, act, down):
    td, tt = (T, D), (T, T)
    (a1b,) = front(xb, gain1, first)
    r1 = swap(a1b)
    (a1a,) = front(xa, gain1, first)
    m1t, m2, m2t, m3, m3t, m4, m4t = call(
        k_prep, [(tt, BF, r) for r in "hvhvhhh"], *h(first, second, third, fourth)
    )
    send2, a2b = call(k_mid, [((T, 2 * D), BF, "c"), (td, F32, "h")], *v(r1, m2, spec, m3), *h(a1a))
    r2 = swap(send2)
    n1b, gateb, dhid, xb_v, m4_v = call(
        k_ahead,
        [(td, BF, "h"), (td, F32, "v"), ((T, FF), BF, "h"), (td, BF, "v"), (tt, BF, "v")],
        *h(xb, gain1, mix, g, down, m4),
    )
    send3, dy1, dgate, n2, hs, dup, dact = call(
        k_tail_back,
        [((T, 2 * D), BF, "c")]
        + [(td, BF, "h")] * 3
        + [((T, FF), BF, "h")]
        + [((T, FF), BF, "c")] * 2,
        *v(r2, m4_v, xb_v, gateb),
        *h(gain2, m2, spec, m3, up, act, dhid, g, m4t),
        scratch=[pltpu.VMEM(td, F32)] * 3
        + [pltpu.VMEM((2, T, HB), F32)] * 2
        + [pltpu.VMEM(td, BF), pltpu.VMEM((T, 1), F32)],
    )
    r3 = swap(send3)
    keep, other, dn1 = call(
        k_grads,
        [((4, 4, GR, DB), BF, "r"), ((4, 4, GR, DB), BF, "r"), (td, F32, "c")],
        *((w, "x" if w is mix else "c") for w in (n1b, dgate, mix, n2, dup, dact, hs, g)),
        scratch=[pltpu.VMEM((2, 4, 4, GR, DB), BF), pltpu.SemaphoreType.DMA((8,))],
    )
    other = lax.ppermute(other, "seq", [(i, i ^ 1) for i in range(32)])
    s0, *sy, m3t, m2t = call(
        k_sum_core, [((4, GR, DB), BF, "h")] * 4 + [(tt, BF, "v")] * 2,
        *h(keep), *v(other), *h(m3t, m2t),
    )
    for d in (1, 3, 2):
        sy[d - 1] = ring(sy[d - 1], ring_y, ring_x, d)
    da1, sgrad = call(
        k_mid_back, [(td, BF, "c")] * 2, *v(r3, m3t), (a2b, "c"), *v(spec, m2t),
        scratch=[pltpu.VMEM(td, F32)],
    )
    r4 = swap(da1)
    (outa,) = call(
        k_tail, [(td, BF, "v")], *h(r3, m4, xa, gain1, mix, gain2, up, act, down),
        scratch=[pltpu.VMEM(td, F32), pltpu.VMEM(td, BF), pltpu.VMEM((T, FF), BF)]
        + [pltpu.VMEM(td, F32)] * 2
        + [pltpu.VMEM((2, T, HB), F32)] * 2,
    )
    next_input = shift(outa, 1)
    (dx,) = call(
        k_end, [(td, BF, "v")], *v(r4), *h(m1t, xb, gain1, dn1, dy1),
        scratch=[pltpu.VMEM(td, F32)],
    )
    upstream = shift(dx, -1)
    s0, *sx = call(k_sum_ring, [((GR, DB), BF, r) for r in "hvvv"], *h(s0), *v(*sy))
    sx = [ring(p, ring_x, ring_y, d + 1) for d, p in enumerate(sx)]
    gm, gu, ga, gd = call(
        k_sum_x,
        [((32, DB), BF, "h"), ((32, HB), BF, "h"), ((32, HB), BF, "h"), ((64, DB), BF, "h")],
        *h(s0), *v(*sx),
    )
    next_input, upstream = call(
        k_place, [((1, T, D), BF, "r")] * 2, *v(next_input, upstream),
        scratch=[pltpu.VMEM(td, BF), pltpu.SemaphoreType.DMA((2,))],
    )
    return (
        next_input,
        upstream,
        sgrad.reshape(1, NI, 4, D),
        gm[None],
        gu[None],
        ga[None],
        gd[None],
    )


def solution(mesh):
    in_specs = (
        P("section", "seq", None),
        P("section", "seq", None),
        P("section", "seq", None),
        P("section", None),
        P("section", None),
        P("section", "seq", None, None),
        P("section", "seq", None, None),
        P("section", None, "seq", None),
        P("section", "seq", None, None),
        P("section", "seq", None, None),
        P("section", None, None),
        P("section", None, None),
        P("section", None, None),
        P("section", None, None),
    )
    out_specs = (
        P("section", "seq", None),
        P("section", "seq", None),
        P("section", None, "seq", None),
        P("section", "seq", None),
        P("section", "seq", None),
        P("section", "seq", None),
        P("section", "seq", None),
    )
    return jax.shard_map(shards, mesh=mesh, in_specs=in_specs, out_specs=out_specs, check_vma=False)
```
